256 devices in a mesh: fsdp: 16 (over z, x_hi), dp: 16 (over y, x_lo, core).
Axes of the slice: x: 4 (x_hi: 2, x_lo: 2; x = x_hi * 2 + x_lo), y: 4, z: 8, core: 2. Of those that a mesh axis runs over, the one named last changes fastest.
Arguments:
- features: bfloat16 [65536, 1024], P(('fsdp', 'dp')), may hold values from -24 to 24
- normed: bfloat16 [65536, 4096], P(('fsdp', 'dp')), may hold values from -6 to 6
- relu_mask: int32 [65536, 4096], P(('fsdp', 'dp')), may hold values 0 or 1
- cotangent: bfloat16 [65536, 4096], P(('fsdp', 'dp')), may hold values from -40 to 40
- weight_shard: bfloat16 [1024, 4096], P('fsdp'), may hold values from -0.1875 to 0.1875
- norm_gain: float32 [4096], replicated, may hold values from 0.25 to 1.75
- inverse_deviation: float32 [4096], replicated, may hold values from 0.5 to 3
Outputs:
- grad_input: bfloat16 [65536, 1024], P(('fsdp', 'dp'))
- grad_weight: float32 [1024, 4096], P('fsdp')
- grad_gain: float32 [4096], replicated
- grad_shift: float32 [4096], replicated
The draws below stay inside these ranges and needn't reach their ends.
All inputs are finite; a program needn't handle non-finite values. No bound on the sum of `relu_mask` on one device may be relied on, other than what follows from the above.
Results may differ from the reference program's by a relative error of at most 0.005.
Values may be sent and summed in bfloat16 or wider, within the bound.
A program may use at most 128 MiB of HBM per device.

```python
import math
import jax
import jax.numpy as jnp
from jax import lax

DIN = 1024
DOUT = 4096
ROWS = 65536


def draw_cotangent(key, part):
    keys = jax.random.split(jax.random.fold_in(key, 11), 3)
    position = jnp.arange(ROWS).astype(jnp.float32) / ROWS
    rising = 3.0 ** position
    column_scale = 10.0 ** jax.random.uniform(keys[1], (DOUT,), jnp.float32)
    row_scale = rising * 10.0 ** (0.5 * jax.random.uniform(keys[0], (ROWS,), jnp.float32))
    noise = jnp.clip(jax.random.normal(keys[2], (ROWS, DOUT), jnp.float32), -4.0, 4.0)
    values = 0.05 * noise * row_scale[:, None] * column_scale[None, :]
    return values.astype(jnp.bfloat16)


def with_ends(values, own_key, low, top_value):
    dims = values.shape
    place = [jax.random.randint(jax.random.fold_in(own_key, axis), (), 0, dims[axis]) for axis in range(len(dims))]
    values = values.at[tuple(place)].set(low)
    longest = dims.index(max(dims))
    place[longest] = (place[longest] + 1) % dims[longest]
    return values.at[tuple(place)].set(top_value)


def with_spikes(drawn, key, source, target, parts, factor):
    owner, partner = [(jnp.arange(drawn.shape[dim]) // (drawn.shape[dim] // parts)).reshape([-1 if axis == dim else 1 for axis in range(drawn.ndim)]) for dim in (source, target)]
    chosen = jax.random.permutation(key, parts)[partner]
    strong = (owner == chosen) | (owner == (partner + parts // 2) % parts)
    return jnp.where(strong, factor * drawn, drawn)


def block_levels(stream_key, dims, cuts, smallest, top_value):
    def one(dim, parts):
        heights = jax.random.uniform(jax.random.fold_in(jax.random.fold_in(stream_key, 6), dim), (parts,), jnp.float32, smallest / len(cuts), top_value / len(cuts))
        return jnp.repeat(jnp.exp(heights), dims[dim] // parts).reshape((-1,) + (1,) * (len(dims) - dim - 1))

    loudness = one(*cuts[0])
    for cut in cuts[1:]:
        loudness = loudness * one(*cut)
    return loudness


def centred(key, shape, width, reach, cuts=(), held_as=jnp.bfloat16):
    factor_of = block_levels(key, shape, cuts, -0.22, 0.18) if cuts else 1.0
    array = jax.random.normal(key, shape, jnp.float32) * width * factor_of
    return jnp.minimum(jnp.maximum(array, -reach), reach).astype(held_as)


def bell_draw_with(stream_key, extent, width, most, cuts, heavy, dtype=jnp.bfloat16):
    result = width * jax.random.normal(stream_key, extent, jnp.float32)
    if cuts:
        result = result * block_levels(stream_key, extent, cuts, -0.22, 0.18)
    return jnp.clip(with_spikes(result, jax.random.fold_in(stream_key, 3), *heavy), -most, most).astype(dtype)


def setup_inputs(seed: int = 0) -> dict:
    key_of = jax.random.split(jax.random.key(seed), 8)
    features = bell_draw_with(key_of[0], (ROWS, DIN), 1.0, 24.0, ((0, 256),), (0, 1, 256, 6.0))
    normed = centred(key_of[1], (ROWS, DOUT), 1.0, 6.0, ((0, 256),))
    relu_mask = with_ends((jax.random.randint(key_of[2], (ROWS, DOUT), 0, 2) < 1).astype(jnp.int32), jax.random.fold_in(key_of[2], 1), 0, 1)
    cotangent = draw_cotangent(jax.random.fold_in(key_of[7], 71), 0)
    weight_shard = centred(key_of[4], (DIN, DOUT), DIN ** -0.5, 0.1875, ((0, 16),))
    norm_gain = jnp.clip(1.0 + 0.15 * jax.random.normal(key_of[5], (DOUT,), jnp.float32), 0.25, 1.75)
    inverse_deviation = jnp.clip(jnp.exp(jax.random.uniform(key_of[6], (DOUT,), jnp.float32, math.log(0.5), math.log(3.0))), 0.5, 3.0)
    return {"features": features, "normed": normed, "relu_mask": relu_mask, "cotangent": cotangent, "weight_shard": weight_shard, "norm_gain": norm_gain, "inverse_deviation": inverse_deviation}


def reference(features, normed, relu_mask, cotangent, weight_shard, norm_gain, inverse_deviation):
    masked = cotangent.astype(jnp.float32) * relu_mask.astype(jnp.float32)
    normed_f = normed.astype(jnp.float32)
    sum_plain = lax.optimization_barrier(jnp.sum(masked, axis=0))
    sum_cross = lax.optimization_barrier(jnp.sum(masked * normed_f, axis=0))
    norm_grad = inverse_deviation * norm_gain * (masked - sum_plain / ROWS - normed_f * (sum_cross / ROWS))
    norm_grad = norm_grad.astype(jnp.bfloat16)
    grad_input = jnp.dot(norm_grad, weight_shard.T, preferred_element_type=jnp.float32).astype(jnp.bfloat16)
    rescale = 1.0 / math.sqrt(ROWS)
    grad_weight = jnp.dot(features.T, norm_grad, preferred_element_type=jnp.float32) * rescale
    return (grad_input, grad_weight, sum_cross * rescale, sum_plain * rescale)
```

```python
import math

import jax
import jax.numpy as jnp
from jax import lax
from jax.experimental import pallas as pl
from jax.experimental.pallas import tpu as pltpu
from jax.sharding import Mesh
from jax.sharding import PartitionSpec as P

Z, XH, Y, XL, C = "z", "xh", "y", "xl", "c"
NZ, NX, NY = 8, 4, 4
F32, BF16 = jnp.float32, jnp.bfloat16

ROWS = 256
DIN = 1024
DOUT = 4096
LANES = 128
BLOCKS = DOUT // LANES
CHUNKS = BLOCKS // (NY * 2)
HALF = BLOCKS // 2
GROUPS = 4

STAGE_X = BF16
STAGE_Z = BF16


def body(
    feat_hbm, normed_hbm, mask_hbm, cot_hbm, w_hbm, gain_hbm, inv_hbm,
    gi_hbm, gw_hbm, stat_hbm,
    feat, normed, mask, cot, scale_a, scale_b, msk, wf, ft, ngs, ngr, rel,
    xs, xr, zs, zr, gw, gi, acc, st, st_core, st_z, st_x, st_y, st_all,
    load_sem, out_sem,
    sc_s, sc_r, sz_s, sz_r, sx_s, sx_r, sy_s, sy_r, sa_s, sa_r,
    f_s, f_r, fp_s, fp_r,
    wo_s, wo_r, wz_s, wz_r, wp_s, wp_r,
    ng_s, ng_r, rl_s, rl_r, fw_s,
    x_s, x_r, z_s, z_r, g_s, g_r, gp_s, gp_r,
):
    z, xh, y, xl, c = (lax.axis_index(name) for name in (Z, XH, Y, XL, C))
    x = 2 * xh + xl
    oc, oxh, oxl = 1 - c, 1 - xh, 1 - xl
    yp, ym, y2 = (y + 1) % NY, (y + 3) % NY, (y + 2) % NY
    zp, zm = (z + 1) % NZ, (z + NZ - 1) % NZ
    me = 2 * y + c
    partner = {C: oc}
    x_peers = [(oxh, oxl), (xh, oxl), (oxh, xl)]
    sent = []

    def send(src, dst, ss, rs, device):
        copy = pltpu.make_async_remote_copy(
            src_ref=src, dst_ref=dst, send_sem=ss, recv_sem=rs,
            device_id=device, device_id_type=pl.DeviceIdType.MESH,
        )
        copy.start()
        sent.append(copy)

    def arrived(dst, ss, rs):
        pltpu.make_async_remote_copy(
            src_ref=dst, dst_ref=dst, send_sem=ss, recv_sem=rs,
            device_id=partner, device_id_type=pl.DeviceIdType.MESH,
        ).wait_recv()

    load_feat = pltpu.make_async_copy(feat_hbm, feat, load_sem.at[0])
    load_w = pltpu.make_async_copy(w_hbm, wf.at[z, xh], load_sem.at[1])
    load_a = pltpu.make_async_copy(gain_hbm, scale_a, load_sem.at[2])
    load_b = pltpu.make_async_copy(inv_hbm, scale_b, load_sem.at[3])
    loads = []
    width = DOUT // GROUPS
    load_feat.start()
    for group in range(GROUPS):
        cols = pl.ds(group * width, width)
        loads.append([
            pltpu.make_async_copy(src.at[:, cols], dst.at[:, cols], load_sem.at[4 + 3 * group + k])
            for k, (src, dst) in enumerate(((cot_hbm, cot), (mask_hbm, mask), (normed_hbm, normed)))
        ])
        for copy in loads[-1]:
            copy.start()
    load_w.start()
    load_a.start()
    load_b.start()

    barrier = pltpu.get_barrier_semaphore()
    friends = [partner]
    for other in (yp, ym, y2):
        friends += [{Y: other, C: c}, {Y: other, C: oc}, {Y: other, XL: oxl}]
    friends += [{XH: a, XL: b} for a, b in x_peers]
    friends += [{Z: (z + k) % NZ} for k in range(1, NZ)]
    for friend in friends:
        pl.semaphore_signal(barrier, inc=1, device_id=friend, device_id_type=pl.DeviceIdType.MESH)

    load_feat.wait()
    for k in range(DIN // LANES):
        part = feat[:, k * LANES:(k + 1) * LANES]
        ft[me, k * LANES:(k + 1) * LANES, :] = part.T

    pl.semaphore_wait(barrier, len(friends))

    send(ft.at[me], ft.at[me], f_s.at[0], f_r.at[0], {Y: yp})
    send(ft.at[me], ft.at[me], f_s.at[1], f_r.at[1], {Y: ym})
    load_w.wait()
    outer = {XH: oxh, XL: oxl}
    send(wf.at[z, xh, c], wf.at[z, xh, c], wo_s.at[0], wo_r.at[0], outer)

    per_group = BLOCKS // GROUPS
    for group in range(GROUPS):
        for copy in loads[group]:
            copy.wait()

        def sums(i, carry):
            b = group * per_group + i
            cols = pl.ds(pl.multiple_of(b * LANES, LANES), LANES)
            value = jnp.where(mask[:, cols] != 0, cot[:, cols].astype(F32), 0.0)
            msk[b] = value.astype(BF16)
            half, row = b // HALF, b % HALF
            st[half, pl.ds(row, 1), :] = jnp.sum(value, axis=0, keepdims=True)
            cross = value * normed[:, cols].astype(F32)
            st[half, pl.ds(HALF + row, 1), :] = jnp.sum(cross, axis=0, keepdims=True)
            return carry

        lax.fori_loop(0, per_group, sums, 0)

    send(st.at[oc], st_core.at[c], sc_s.at[0], sc_r.at[0], partner)
    arrived(st_core.at[oc], sc_s.at[0], sc_r.at[0])
    st_core[c] = st[c]
    st_z[z] = st_core[0] + st_core[1]
    for k in range(1, NZ):
        send(st_z.at[z], st_z.at[z], sz_s.at[k], sz_r.at[z], {Z: (z + k) % NZ})

    def other(o):
        return xh if o == 0 else oxh

    def weights_on(direction, step, o):
        block = (z - (step - 1)) % NZ if direction == 0 else (z + (step - 1)) % NZ
        ref = wf.at[block, other(o), c]
        send(ref, ref, wz_s.at[direction, step - 1, o], wz_r.at[direction, step - 1, o],
             {Z: zp if direction == 0 else zm})

    def weights_in(direction, step, o):
        block = (z - step + NZ) % NZ if direction == 0 else (z + step) % NZ
        ref = wf.at[block, other(o), c]
        arrived(ref, wz_s.at[direction, step - 1, o], wz_r.at[direction, step - 1, o])
        send(ref, ref, wp_s.at[direction, step - 1, o], wp_r.at[direction, step - 1, o], partner)

    def weights_over(direction, step, o):
        block = (z - step + NZ) % NZ if direction == 0 else (z + step) % NZ
        ref = wf.at[block, other(o), oc]
        arrived(ref, wp_s.at[direction, step - 1, o], wp_r.at[direction, step - 1, o])

    def weights_next(step, o):
        for direction in range(2):
            if step == 4:
                if direction == o:
                    weights_in(direction, step, o)
                continue
            block_in = (z - step + NZ) % NZ if direction == 0 else (z + step) % NZ
            ref = wf.at[block_in, other(o), c]
            arrived(ref, wz_s.at[direction, step - 1, o], wz_r.at[direction, step - 1, o])
            if step < 3 or direction == o:
                send(ref, ref, wz_s.at[direction, step, o], wz_r.at[direction, step, o],
                     {Z: zp if direction == 0 else zm})
            send(ref, ref, wp_s.at[direction, step - 1, o], wp_r.at[direction, step - 1, o], partner)

    weights_on(0, 1, 0)
    weights_on(1, 1, 0)
    arrived(wf.at[z, oxh, c], wo_s.at[0], wo_r.at[0])
    weights_on(0, 1, 1)
    weights_on(1, 1, 1)
    send(wf.at[z, oxh, c], wf.at[z, oxh, c], wp_s.at[0, 3, 1], wp_r.at[0, 3, 1], partner)

    for k in range(1, NZ):
        source = (z + k) % NZ
        arrived(st_z.at[source], sz_s.at[k], sz_r.at[source])
    st_x[x] = sum((st_z[k] for k in range(1, NZ)), st_z[0])
    for k, (a, b) in enumerate(x_peers):
        send(st_x.at[x], st_x.at[x], sx_s.at[k], sx_r.at[x], {XH: a, XL: b})
    for k, (a, b) in enumerate(x_peers):
        source = 2 * a + b
        arrived(st_x.at[source], sx_s.at[k], sx_r.at[source])
    st_y[y] = st_x[0] + st_x[1] + st_x[2] + st_x[3]
    for k in range(1, NY):
        send(st_y.at[y], st_y.at[y], sy_s.at[k], sy_r.at[y], {Y: (y + k) % NY})

    mid = DIN // 2
    send(ft.at[me], ft.at[me], fp_s.at[0], fp_r.at[0], partner)
    low, high = ft.at[2 * ym + c], ft.at[2 * yp + c]
    arrived(low, f_s.at[0], f_r.at[0])
    part = ft.at[2 * ym + c, pl.ds(0, mid)]
    send(part, part, f_s.at[2], f_r.at[2], {Y: yp})
    arrived(high, f_s.at[1], f_r.at[1])
    part = ft.at[2 * yp + c, pl.ds(mid, mid)]
    send(part, part, f_s.at[3], f_r.at[3], {Y: ym})
    send(low, low, fp_s.at[1], fp_r.at[1], partner)
    send(high, high, fp_s.at[2], fp_r.at[2], partner)

    for k in range(1, NY):
        source = (y + k) % NY
        arrived(st_y.at[source], sy_s.at[k], sy_r.at[source])
    st_all[c] = st_y[0] + st_y[1] + st_y[2] + st_y[3]
    send(st_all.at[c], st_all.at[c], sa_s.at[0], sa_r.at[0], partner)
    load_a.wait()
    load_b.wait()
    arrived(st_all.at[oc], sa_s.at[0], sa_r.at[0])
    store_stat = pltpu.make_async_copy(st_all, stat_hbm, out_sem.at[0])
    store_stat.start()

    inverse_rows = 1.0 / (ROWS * NZ * NX * NY * 2)

    def norm_grad(j):
        def one(i, carry):
            b = i * CHUNKS + j
            cols = pl.ds(pl.multiple_of(b * LANES, LANES), LANES)
            half, row = b // HALF, b % HALF
            plain = st_all[half, pl.ds(row, 1), :] * inverse_rows
            cross = st_all[half, pl.ds(HALF + row, 1), :] * inverse_rows
            scale = scale_b[pl.ds(b, 1), :] * scale_a[pl.ds(b, 1), :]
            value = msk[b].astype(F32) - plain - normed[:, cols].astype(F32) * cross
            ngs[b] = (scale * value).astype(BF16)
            return carry

        lax.fori_loop(0, NY * 2, one, 0)
        ngr[j, me] = ngs[me * CHUNKS + j]

    def block(chip, core, j):
        return ngs.at[(chip * 2 + core) * CHUNKS + j]

    def send_far(j):
        send(block(y2, 0, j), rel.at[0, j], rl_s.at[0, j], rl_r.at[0, j], {Y: yp})
        send(block(y2, 1, j), rel.at[1, j], rl_s.at[1, j], rl_r.at[1, j], {Y: ym})

    def send_near(j):
        for k, chip in enumerate((yp, ym)):
            for core in range(2):
                send(block(chip, core, j), ngr.at[j, me], ng_s.at[j, 2 * k + core], ng_r.at[j, me],
                     {Y: chip, C: core})
        send(block(y, oc, j), ngr.at[j, me], ng_s.at[j, 4], ng_r.at[j, me], partner)

    def pass_on(j):
        arrived(rel.at[0, j], rl_s.at[0, j], rl_r.at[0, j])
        source = 2 * ym + c
        send(rel.at[0, j], ngr.at[j, source], fw_s.at[0, j], ng_r.at[j, source], {Y: yp, C: 0})
        arrived(rel.at[1, j], rl_s.at[1, j], rl_r.at[1, j])
        source = 2 * yp + c
        send(rel.at[1, j], ngr.at[j, source], fw_s.at[1, j], ng_r.at[j, source], {Y: ym, C: 1})

    def multiply(j):
        for k in range(1, NY * 2):
            source = (me + k) % (NY * 2)
            arrived(ngr.at[j, source], ng_s.at[j, 0], ng_r.at[j, source])
        tall = 256

        def tile(i, carry):
            rows = pl.ds(pl.multiple_of(i * tall, tall), tall)
            left = jnp.concatenate([ft[s, rows, :] for s in range(NY * 2)], axis=1)
            right = jnp.concatenate([ngr[j, s] for s in range(NY * 2)], axis=0)
            out = jnp.dot(left, right, preferred_element_type=F32).astype(STAGE_X)
            each = DIN // NZ
            share = each // NX
            for a in range(tall // each):
                for b in range(NX):
                    xs[j, b, i * (tall // each) + a] = out[a * each + b * share:a * each + (b + 1) * share]
            return carry

        lax.fori_loop(0, DIN // tall, tile, 0)
        for k, (a, b) in enumerate(x_peers):
            send(xs.at[j, 2 * a + b], xr.at[j, x], x_s.at[j, k], x_r.at[j, x], {XH: a, XL: b})
        xr[j, x] = xs[j, x]

    def over_x(j):
        for k, (a, b) in enumerate(x_peers):
            source = 2 * a + b
            arrived(xr.at[j, source], x_s.at[j, k], x_r.at[j, source])
        total = xr[j, 0].astype(F32)
        for k in range(1, NX):
            total += xr[j, k].astype(F32)
        zs[j] = total.astype(STAGE_Z)
        for k in range(1, NZ):
            to = (z + k) % NZ
            send(zs.at[j, to], zr.at[j, z], z_s.at[j, k], z_r.at[j, z], {Z: to})
        zr[j, z] = zs[j, z]

    def over_z(j):
        for k in range(1, NZ):
            source = (z + k) % NZ
            arrived(zr.at[j, source], z_s.at[j, k], z_r.at[j, source])
        total = zr[j, 0].astype(F32)
        for k in range(1, NZ):
            total += zr[j, k].astype(F32)
        gw[xl, y, c, j] = total
        mine = gw.at[xl, y, c, j]
        k = 0
        for chip in (yp, ym, y2, y):
            for side in (oxl, xl):
                if chip is y and side is xl:
                    continue
                send(mine, mine, g_s.at[j, k], g_r.at[j, xl * NY + y], {Y: chip, XL: side})
                k += 1

    def gathered(j):
        for chip in (yp, ym, y2, y):
            for side in (oxl, xl):
                if chip is y and side is xl:
                    continue
                arrived(gw.at[side, chip, c, j], g_s.at[j, 0], g_r.at[j, side * NY + chip])
        part = gw.at[:, :, c, j]
        send(part, part, gp_s.at[j], gp_r.at[j], partner)

    def grad_input(p):
        acc[...] = jnp.zeros_like(acc)
        deep = 1024

        def step(i, carry):
            cols = pl.ds(pl.multiple_of(i * deep, deep), deep)
            count = deep // LANES
            left = jnp.concatenate([ngs[i * count + k] for k in range(count)], axis=1)
            right = wf[2 * p:2 * p + 2, :, :, :, cols].reshape(256, deep)
            acc[...] += lax.dot_general(left, right, (((1,), (1,)), ((), ())), preferred_element_type=F32)
            return carry

        lax.fori_loop(0, DOUT // deep, step, 0)
        gi[:, p * 256:(p + 1) * 256] = acc[...].astype(BF16)

    norm_grad(0)
    send_far(0)
    send_near(0)
    norm_grad(1)
    send_far(1)
    weights_next(1, 0)
    for j in range(CHUNKS):
        pass_on(j)
        if j + 1 < CHUNKS:
            send_near(j + 1)
        if j + 2 < CHUNKS:
            norm_grad(j + 2)
            send_far(j + 2)
        if j == 0:
            weights_next(1, 1)
            far = ft.at[2 * y2 + c]
            arrived(ft.at[2 * y2 + c, pl.ds(0, mid)], f_s.at[2], f_r.at[2])
            arrived(ft.at[2 * y2 + c, pl.ds(mid, mid)], f_s.at[3], f_r.at[3])
            send(far, far, fp_s.at[3], fp_r.at[3], partner)
            for k, chip in enumerate((y, ym, yp, y2)):
                arrived(ft.at[2 * chip + oc], fp_s.at[k], fp_r.at[k])
        multiply(j)
        if j >= 1:
            over_x(j - 1)
        if j >= 2:
            over_z(j - 2)
        if j >= 3:
            gathered(j - 3)
        if j == 0:
            weights_next(2, 0)
        if j == 1:
            weights_next(2, 1)
        if j == 2:
            weights_next(3, 0)
    weights_next(3, 1)
    over_x(3)
    over_z(2)
    gathered(1)
    weights_next(4, 0)
    weights_next(4, 1)
    arrived(wf.at[z, oxh, oc], wp_s.at[0, 3, 1], wp_r.at[0, 3, 1])
    for step in range(1, 5):
        for o in range(2):
            for direction in range(2):
                if step < 4 or direction == o:
                    weights_over(direction, step, o)
    grad_input(0)
    grad_input(1)
    over_z(3)
    gathered(2)
    grad_input(2)
    grad_input(3)
    store_gi = pltpu.make_async_copy(gi, gi_hbm, out_sem.at[1])
    store_gi.start()
    gathered(3)
    for j in range(CHUNKS):
        arrived(gw.at[:, :, oc, j], gp_s.at[j], gp_r.at[j])
    store_gw = pltpu.make_async_copy(gw, gw_hbm, out_sem.at[2])
    store_gw.start()
    for copy in sent:
        copy.wait_send()
    store_stat.wait()
    store_gi.wait()
    store_gw.wait()


def on_device(features, normed, relu_mask, cotangent, weight_shard, norm_gain, inverse_deviation):
    dma = pltpu.SemaphoreType.DMA
    vmem = pltpu.VMEM
    any_space = pl.BlockSpec(memory_space=pl.ANY)
    rows_out = DIN // (NZ * NX)
    scratch = [
        vmem((ROWS, DIN), BF16), vmem((ROWS, DOUT), BF16), vmem((ROWS, DOUT), jnp.int32), vmem((ROWS, DOUT), BF16),
        vmem((BLOCKS, LANES), F32), vmem((BLOCKS, LANES), F32), vmem((BLOCKS, ROWS, LANES), BF16),
        vmem((NZ, 2, 2, 32, DOUT), BF16), vmem((NY * 2, DIN, ROWS), BF16),
        vmem((BLOCKS, ROWS, LANES), BF16), vmem((CHUNKS, NY * 2, ROWS, LANES), BF16), vmem((2, CHUNKS, ROWS, LANES), BF16),
        vmem((CHUNKS, NX, NZ, rows_out, LANES), STAGE_X), vmem((CHUNKS, NX, NZ, rows_out, LANES), STAGE_X),
        vmem((CHUNKS, NZ, rows_out, LANES), STAGE_Z), vmem((CHUNKS, NZ, rows_out, LANES), STAGE_Z),
        vmem((2, NY, 2, CHUNKS, rows_out, LANES), F32), vmem((ROWS, DIN), BF16), vmem((ROWS, 256), F32),
        vmem((2, BLOCKS, LANES), F32), vmem((2, BLOCKS, LANES), F32), vmem((NZ, BLOCKS, LANES), F32),
        vmem((NX, BLOCKS, LANES), F32), vmem((NY, BLOCKS, LANES), F32), vmem((2, BLOCKS, LANES), F32),
        dma((4 + 3 * GROUPS,)), dma((3,)),
        dma((1,)), dma((1,)), dma((NZ,)), dma((NZ,)), dma((3,)), dma((NX,)), dma((NY,)), dma((NY,)), dma((1,)), dma((1,)),
        dma((4,)), dma((4,)), dma((4,)), dma((4,)),
        dma((1,)), dma((1,)), dma((2, 4, 2)), dma((2, 4, 2)), dma((2, 4, 2)), dma((2, 4, 2)),
        dma((CHUNKS, 5)), dma((CHUNKS, NY * 2)), dma((2, CHUNKS)), dma((2, CHUNKS)), dma((2, CHUNKS)),
        dma((CHUNKS, 3)), dma((CHUNKS, NX)), dma((CHUNKS, NZ)), dma((CHUNKS, NZ)),
        dma((CHUNKS, 7)), dma((CHUNKS, 2 * NY)), dma((CHUNKS,)), dma((CHUNKS,)),
    ]
    grad_input, pieces, sums = pl.pallas_call(
        body,
        out_shape=(
            jax.ShapeDtypeStruct((ROWS, DIN), BF16),
            jax.ShapeDtypeStruct((2, NY, 2, CHUNKS, rows_out, LANES), F32),
            jax.ShapeDtypeStruct((2, BLOCKS, LANES), F32),
        ),
        in_specs=[any_space] * 7,
        out_specs=(any_space,) * 3,
        scratch_shapes=scratch,
        compiler_params=pltpu.CompilerParams(
            collective_id=0, has_side_effects=True, vmem_limit_bytes=56 * 1024 * 1024,
        ),
    )(
        features, normed, relu_mask, cotangent, weight_shard.reshape(2, 32, DOUT),
        norm_gain.reshape(BLOCKS, LANES), inverse_deviation.reshape(BLOCKS, LANES),
    )
    rescale = 1.0 / math.sqrt(ROWS * NZ * NX * NY * 2)
    grad_weight = pieces.reshape(2, BLOCKS, rows_out, LANES).transpose(0, 2, 1, 3).reshape(2 * rows_out, DOUT) * rescale
    sums = sums.reshape(2, 2, DOUT // 2) * rescale
    return grad_input, grad_weight, sums[:, 1].reshape(DOUT), sums[:, 0].reshape(DOUT)


def solution(mesh):
    split = Mesh(mesh.devices.reshape(NZ, 2, NY, 2, 2), (Z, XH, Y, XL, C))
    rows = P((Z, XH, Y, XL, C), None)
    shard = P((Z, XH), None)
    return jax.shard_map(
        on_device,
        mesh=split,
        in_specs=(rows, rows, rows, rows, shard, P(), P()),
        out_specs=(rows, shard, P(), P()),
        check_vma=False,
    )
```

```python
import functools
import math

import jax
import jax.numpy as jnp
from jax import lax
from jax.experimental import pallas as pl
from jax.experimental.pallas import tpu as pltpu
from jax.sharding import Mesh
from jax.sharding import PartitionSpec as P

Z, XH, Y, XL, C = "z", "xh", "y", "xl", "c"
NZ, NX, NY = 8, 4, 4
F32, BF16 = jnp.float32, jnp.bfloat16

ROWS = 256
DIN = 1024
DOUT = 4096
LANES = 128
BLOCKS = DOUT // LANES
CHUNKS = BLOCKS // (NY * 2)
HALF = BLOCKS // 2
GROUPS = 4

STAGE_X = BF16
STAGE_Z = BF16


def body(
    feat_hbm, normed_hbm, mask_hbm, cot_hbm, w_hbm, gain_hbm, inv_hbm,
    gi_hbm, gw_hbm, stat_hbm,
    feat, normed, mask, cot, scale_a, scale_b, msk, wf, ft, ngs, ngr, rel,
    xs, xr, zs, zr, gw, gi, acc, near, st, st_core, st_x, st_y, st_z, st_all,
    load_sem, out_sem, stat_s, stat_r,
    f_s, f_r, fp_s, fp_r,
    wo_s, wo_r, wz_s, wz_r, wl_r, wp_s, wp_r,
    ng_s, near_r, far_r, rel_r,
    x_s, x_r, z_s, z_r, g_s, g_r, gp_s, gp_r,
):
    z, xh, y, xl, c = (lax.axis_index(name) for name in (Z, XH, Y, XL, C))
    x = 2 * xh + xl
    oc, oxh, oxl = 1 - c, 1 - xh, 1 - xl
    yp, ym, y2 = (y + 1) % NY, (y + 3) % NY, (y + 2) % NY
    zp, zm = (z + 1) % NZ, (z + NZ - 1) % NZ
    me = 2 * y + c
    partner = {C: oc}
    x_peers = [(oxh, xl), (oxh, oxl), (xh, oxl)]

    def remote(src, dst, ss, rs, device):
        return pltpu.make_async_remote_copy(
            src_ref=src, dst_ref=dst, send_sem=ss, recv_sem=rs,
            device_id=device, device_id_type=pl.DeviceIdType.MESH,
        )

    def send(src, dst, ss, rs, device):
        remote(src, dst, ss, rs, device).start()

    def arrived(ref, rs):
        remote(ref, ref, rs, rs, partner).wait_recv()

    def left(ref, ss):
        remote(ref, ref, ss, ss, partner).wait_send()

    load_feat = pltpu.make_async_copy(feat_hbm, feat, load_sem.at[0])
    load_w = pltpu.make_async_copy(w_hbm, wf.at[z, xh], load_sem.at[1])
    load_a = pltpu.make_async_copy(gain_hbm, scale_a, load_sem.at[2])
    load_b = pltpu.make_async_copy(inv_hbm, scale_b, load_sem.at[3])
    loads = []
    width = DOUT // GROUPS
    load_feat.start()
    load_w.start()
    for group in range(GROUPS):
        cols = pl.ds(group * width, width)
        loads.append([
            pltpu.make_async_copy(src.at[:, cols], dst.at[:, cols], load_sem.at[4 + 3 * group + k])
            for k, (src, dst) in enumerate(((cot_hbm, cot), (mask_hbm, mask), (normed_hbm, normed)))
        ])
        for copy in loads[-1]:
            copy.start()
    load_a.start()
    load_b.start()

    barrier = pltpu.get_barrier_semaphore()
    friends = [partner]
    for other in (yp, ym, y2):
        friends += [{Y: other, C: c}, {Y: other, C: oc}, {Y: other, XL: oxl}]
    friends += [{XH: a, XL: b} for a, b in x_peers]
    friends += [{Z: (z + k) % NZ} for k in range(1, NZ)]
    for friend in friends:
        pl.semaphore_signal(barrier, inc=1, device_id=friend, device_id_type=pl.DeviceIdType.MESH)

    load_feat.wait()
    for k in range(DIN // LANES):
        part = feat[:, k * LANES:(k + 1) * LANES]
        ft[me, k * LANES:(k + 1) * LANES, :] = part.T

    pl.semaphore_wait(barrier, len(friends))

    quarter = DIN // 4

    def feature(direction, q, late):
        ref = ft.at[me, pl.ds(q * quarter, quarter)]
        send(ref, ref, f_s.at[direction], f_r.at[late, direction], {Y: yp if direction == 0 else ym})

    feature(0, 0, 0)
    feature(1, 2, 0)
    def side(o):
        return xh if o == 0 else oxh

    def weights_on(direction, block, step, o):
        ref = wf.at[block, side(o), c]
        send(ref, ref, wz_s.at[0], wz_r.at[direction, step - 1, o], {Z: zp if direction == 0 else zm})

    def weights_next(step, o):
        blocks = [(z + NZ - step) % NZ, (z + step) % NZ]
        for direction, b in enumerate(blocks):
            arrived(wf.at[b, side(o), c], wz_r.at[direction, step - 1, o])
            if step < 3:
                weights_on(direction, b, step + 1, o)
        if step == 3:
            ref = wf.at[(z + 5 - 2 * c) % NZ, side(o), c]
            send(ref, ref, wz_s.at[0], wl_r.at[o], {Z: (z + 1 + 6 * c) % NZ})
        for b in blocks:
            ref = wf.at[b, side(o), c]
            send(ref, ref, wp_s.at[0], wp_r.at[step - 1], partner)

    def weights_last(o):
        ref = wf.at[(z + 4) % NZ, side(o), c]
        arrived(ref, wl_r.at[o])
        send(ref, ref, wp_s.at[0], wp_r.at[3], partner)

    load_w.wait()
    weights_on(0, z, 1, 0)
    weights_on(1, z, 1, 0)

    per_group = BLOCKS // GROUPS
    for group in range(GROUPS):
        for copy in loads[group]:
            copy.wait()

        def sums(i, carry):
            b = group * per_group + i
            cols = pl.ds(pl.multiple_of(b * LANES, LANES), LANES)
            value = jnp.where(mask[:, cols] != 0, cot[:, cols].astype(F32), 0.0)
            msk[b] = value.astype(BF16)
            half, row = b // HALF, b % HALF
            st[half, pl.ds(row, 1), :] = jnp.sum(value, axis=0, keepdims=True)
            cross = value * normed[:, cols].astype(F32)
            st[half, pl.ds(HALF + row, 1), :] = jnp.sum(cross, axis=0, keepdims=True)
            return carry

        lax.fori_loop(0, per_group, sums, 0)

    send(st.at[oc], st_core.at[c], stat_s.at[0], stat_r.at[0], partner)
    arrived(st_core.at[oc], stat_r.at[0])
    st_y[y] = st[c] + st_core[oc]
    for k in (2, 1, 3):
        send(st_y.at[y], st_y.at[y], stat_s.at[1], stat_r.at[1], {Y: (y + k) % NY})
    feature(0, 1, 0)
    feature(1, 3, 0)
    for late in ((2, 1), (3, 0)):
        for direction in range(2):
            feature(direction, late[direction], 1)
    arrived(st_y.at[pl.ds(0, NY - 1)], stat_r.at[1])
    st_x[x] = st_y[0] + st_y[1] + st_y[2] + st_y[3]
    for a, b in x_peers:
        send(st_x.at[x], st_x.at[x], stat_s.at[2], stat_r.at[2], {XH: a, XL: b})
    outer = {XH: oxh, XL: oxl}
    send(wf.at[z, xh, c], wf.at[z, xh, c], wo_s.at[0], wo_r.at[0], outer)
    weights_next(1, 0)
    arrived(st_x.at[pl.ds(0, NX - 1)], stat_r.at[2])
    st_z[z] = st_x[0] + st_x[1] + st_x[2] + st_x[3]
    for k in (4, 3, 5, 2, 6, 1, 7):
        send(st_z.at[z], st_z.at[z], stat_s.at[3], stat_r.at[3], {Z: (z + k) % NZ})
    mid = DIN // 2
    low, high = ft.at[2 * ym + c, pl.ds(0, mid)], ft.at[2 * yp + c, pl.ds(mid, mid)]
    arrived(low, f_r.at[0, 0])
    send(low, low, f_s.at[2], f_r.at[2, 0], {Y: yp})
    arrived(high, f_r.at[0, 1])
    send(high, high, f_s.at[3], f_r.at[2, 1], {Y: ym})
    far_out = wf.at[z, oxh, c]
    arrived(far_out, wo_r.at[0])
    weights_on(0, z, 1, 1)
    weights_on(1, z, 1, 1)
    weights_next(2, 0)
    send(far_out, far_out, wp_s.at[1], wp_r.at[3], partner)
    arrived(st_z.at[pl.ds(0, NZ - 1)], stat_r.at[3])
    st_all[c] = sum((st_z[k] for k in range(1, NZ)), st_z[0])
    send(st_all.at[c], st_all.at[c], stat_s.at[4], stat_r.at[4], partner)
    send(ft.at[me], ft.at[me], fp_s.at[0], fp_r.at[0], partner)
    load_a.wait()
    load_b.wait()
    arrived(st_all.at[oc], stat_r.at[4])
    store_stat = pltpu.make_async_copy(st_all, stat_hbm, out_sem.at[0])
    store_stat.start()

    inverse_rows = 1.0 / (ROWS * NZ * NX * NY * 2)

    def norm_grad(j):
        def one(i, carry):
            b = i * CHUNKS + j
            cols = pl.ds(pl.multiple_of(b * LANES, LANES), LANES)
            half, row = b // HALF, b % HALF
            plain = st_all[half, pl.ds(row, 1), :] * inverse_rows
            cross = st_all[half, pl.ds(HALF + row, 1), :] * inverse_rows
            scale = scale_b[pl.ds(b, 1), :] * scale_a[pl.ds(b, 1), :]
            value = msk[b].astype(F32) - plain - normed[:, cols].astype(F32) * cross
            ngs[b] = (scale * value).astype(BF16)
            return carry

        lax.fori_loop(0, NY * 2, one, 0)
        ngr[j, me] = ngs[me * CHUNKS + j]

    def block(chip, core, j):
        return ngs.at[(chip * 2 + core) * CHUNKS + j]

    def send_far(j):
        send(block(y2, 0, j), rel.at[0, j], ng_s.at[j], rel_r.at[0, j], {Y: yp})
        send(block(y2, 1, j), rel.at[1, j], ng_s.at[j], rel_r.at[1, j], {Y: ym})

    def send_near(j):
        for core in range(2):
            for chip in (yp, ym):
                send(block(chip, core, j), ngr.at[j, me], ng_s.at[j], near_r.at[j], {Y: chip, C: core})
        send(block(y, oc, j), ngr.at[j, me], ng_s.at[j], near_r.at[j], partner)

    def pass_on(j):
        arrived(rel.at[0, j], rel_r.at[0, j])
        send(rel.at[0, j], ngr.at[j, 2 * ym + c], ng_s.at[j], far_r.at[j], {Y: yp, C: 0})
        arrived(rel.at[1, j], rel_r.at[1, j])
        send(rel.at[1, j], ngr.at[j, 2 * yp + c], ng_s.at[j], far_r.at[j], {Y: ym, C: 1})

    tall = 256

    def product(j, rows, sources):
        a = jnp.concatenate([ft[s, rows, :] for s in sources], axis=1)
        b = jnp.concatenate([ngr[j, s] for s in sources], axis=0)
        return jnp.dot(a, b, preferred_element_type=F32)

    def multiply_near(j):
        arrived(ngr.at[j, pl.ds(0, 5)], near_r.at[j])

        def tile(i, carry):
            rows = pl.ds(pl.multiple_of(i * tall, tall), tall)
            near[rows, :] = product(j, rows, [2 * chip + core for chip in (y, yp, ym) for core in range(2)])
            return carry

        lax.fori_loop(0, DIN // tall, tile, 0)

    def multiply_far(j):
        arrived(ngr.at[j, pl.ds(0, 2)], far_r.at[j])

        def tile(i, carry):
            rows = pl.ds(pl.multiple_of(i * tall, tall), tall)
            out = (near[rows, :] + product(j, rows, [2 * y2, 2 * y2 + 1])).astype(STAGE_X)
            each = DIN // NZ
            share = each // NX
            for a in range(tall // each):
                for b in range(NX):
                    xs[j, b, i * (tall // each) + a] = out[a * each + b * share:a * each + (b + 1) * share]
            return carry

        lax.fori_loop(0, DIN // tall, tile, 0)
        for a, b in x_peers:
            send(xs.at[j, 2 * a + b], xr.at[j, x], x_s.at[j], x_r.at[j], {XH: a, XL: b})
        xr[j, x] = xs[j, x]

    def over_x(j):
        arrived(xr.at[j, pl.ds(0, NX - 1)], x_r.at[j])
        total = xr[j, 0].astype(F32)
        for k in range(1, NX):
            total += xr[j, k].astype(F32)
        zs[j] = total.astype(STAGE_Z)
        for k in (4, 3, 5, 2, 6, 1, 7):
            to = (z + k) % NZ
            send(zs.at[j, to], zr.at[j, z], z_s.at[j], z_r.at[j], {Z: to})
        zr[j, z] = zs[j, z]

    others = [(chip, lane) for chip in (y2, yp, ym) for lane in (oxl, xl)] + [(y, oxl)]

    def over_z(j):
        arrived(zr.at[j, pl.ds(0, NZ - 1)], z_r.at[j])
        total = zr[j, 0].astype(F32)
        for k in range(1, NZ):
            total += zr[j, k].astype(F32)
        gw[xl, y, c, j] = total
        mine = gw.at[xl, y, c, j]
        for chip, lane in others:
            send(mine, mine, g_s.at[j], g_r.at[j], {Y: chip, XL: lane})

    def gathered(j):
        arrived(near.at[pl.ds(0, len(others) * 32)], g_r.at[j])
        part = gw.at[:, :, c, j]
        send(part, part, gp_s.at[0], gp_r.at[j], partner)

    def grad_input(step):
        if step == 4:
            arrived(wf.at[pl.ds(0, 3), 0, 0], wp_r.at[3])
            blocks = (z, (z + 4) % NZ)
        else:
            arrived(wf.at[pl.ds(0, 2), :, 0], wp_r.at[step - 1])
            blocks = ((z - step + NZ) % NZ, (z + step) % NZ)
        acc[...] = jnp.zeros_like(acc)
        deep = 1024

        def part(i, carry):
            cols = pl.ds(pl.multiple_of(i * deep, deep), deep)
            count = deep // LANES
            a = jnp.concatenate([ngs[i * count + k] for k in range(count)], axis=1)
            b = jnp.concatenate([wf[k, :, :, :, cols].reshape(LANES, deep) for k in blocks], axis=0)
            acc[...] += lax.dot_general(a, b, (((1,), (1,)), ((), ())), preferred_element_type=F32)
            return carry

        lax.fori_loop(0, DOUT // deep, part, 0)
        for k, place in enumerate(blocks):
            cols = pl.ds(pl.multiple_of(place * LANES, LANES), LANES)
            gi[:, cols] = acc[:, k * LANES:(k + 1) * LANES].astype(BF16)

    def store(j):
        arrived(gw.at[:, :, oc, j], gp_r.at[j])
        copy = pltpu.make_async_copy(gw.at[:, :, :, j], gw_hbm.at[:, :, :, j], out_sem.at[2 + j])
        copy.start()
        return copy

    norm_grad(0)
    send_far(0)
    send_near(0)
    norm_grad(1)
    send_far(1)
    norm_grad(2)
    norm_grad(3)
    arrived(ft.at[2 * ym + c, pl.ds(0, mid)], f_r.at[1, 0])
    arrived(ft.at[2 * yp + c, pl.ds(0, mid)], f_r.at[1, 1])
    for chip in (ym, yp):
        send(ft.at[2 * chip + c], ft.at[2 * chip + c], fp_s.at[0], fp_r.at[0], partner)
    pass_on(0)
    send_far(2)
    send_near(1)
    for direction in range(2):
        arrived(ft.at[2 * y2 + c, pl.ds(direction * mid, mid)], f_r.at[2, direction])
    send(ft.at[2 * y2 + c], ft.at[2 * y2 + c], fp_s.at[0], fp_r.at[0], partner)
    pass_on(1)
    send_far(3)
    send_near(2)
    weights_next(1, 1)
    arrived(ft.at[pl.ds(0, 4)], fp_r.at[0])
    multiply_near(0)
    multiply_far(0)
    pass_on(2)
    send_near(3)
    weights_next(3, 0)
    multiply_near(1)
    multiply_far(1)
    pass_on(3)
    over_x(0)
    weights_next(2, 1)
    grad_input(1)
    multiply_near(2)
    multiply_far(2)
    over_x(1)
    weights_last(0)
    grad_input(2)
    multiply_near(3)
    multiply_far(3)
    over_z(0)
    over_x(2)
    over_z(1)
    weights_next(3, 1)
    grad_input(3)
    over_x(3)
    over_z(2)
    gathered(0)
    gathered(1)
    weights_last(1)
    grad_input(4)
    store_gi = pltpu.make_async_copy(gi, gi_hbm, out_sem.at[1])
    store_gi.start()
    over_z(3)
    gathered(2)
    stores = [store(j) for j in range(CHUNKS - 1)]
    gathered(3)
    stores.append(store(CHUNKS - 1))

    left(st.at[0], stat_s.at[0])
    left(st_y.at[pl.ds(0, NY - 1)], stat_s.at[1])
    left(st_x.at[pl.ds(0, NX - 1)], stat_s.at[2])
    left(st_z.at[pl.ds(0, NZ - 1)], stat_s.at[3])
    left(st.at[0], stat_s.at[4])
    for direction in range(2):
        left(ft.at[0], f_s.at[direction])
        left(low, f_s.at[2 + direction])
    left(ft.at[pl.ds(0, 4)], fp_s.at[0])
    left(far_out, wo_s.at[0])
    left(wf.at[pl.ds(0, 7), :, 0], wz_s.at[0])
    left(wf.at[pl.ds(0, 7), :, 0], wp_s.at[0])
    left(far_out, wp_s.at[1])
    for j in range(CHUNKS):
        left(ngs.at[pl.ds(0, 9)], ng_s.at[j])
        left(xr.at[j, pl.ds(0, NX - 1)], x_s.at[j])
        left(zr.at[j, pl.ds(0, NZ - 1)], z_s.at[j])
        left(near.at[pl.ds(0, len(others) * 32)], g_s.at[j])
    left(gw.at[:, :, c], gp_s.at[0])
    store_stat.wait()
    store_gi.wait()
    for copy in stores:
        copy.wait()


def finish(rescale, gi, gw, stat, gi_out, gw_out, gain, shift):
    gi_out[...] = gi[...]
    tall = gw.shape[2]
    for s in range(2):
        for b in range(BLOCKS):
            gw_out[s * tall:(s + 1) * tall, b * LANES:(b + 1) * LANES] = gw[s, b] * rescale
    for half in range(2):
        rows = slice(half * HALF, (half + 1) * HALF)
        shift[rows, :] = stat[half, :HALF] * rescale
        gain[rows, :] = stat[half, HALF:] * rescale


def on_device(features, normed, relu_mask, cotangent, weight_shard, norm_gain, inverse_deviation):
    dma = pltpu.SemaphoreType.DMA
    vmem = pltpu.VMEM
    any_space = pl.BlockSpec(memory_space=pl.ANY)
    rows_out = DIN // (NZ * NX)
    scratch = [
        vmem((ROWS, DIN), BF16), vmem((ROWS, DOUT), BF16), vmem((ROWS, DOUT), jnp.int32), vmem((ROWS, DOUT), BF16),
        vmem((BLOCKS, LANES), F32), vmem((BLOCKS, LANES), F32), vmem((BLOCKS, ROWS, LANES), BF16),
        vmem((NZ, 2, 2, 32, DOUT), BF16), vmem((NY * 2, DIN, ROWS), BF16),
        vmem((BLOCKS, ROWS, LANES), BF16), vmem((CHUNKS, NY * 2, ROWS, LANES), BF16), vmem((2, CHUNKS, ROWS, LANES), BF16),
        vmem((CHUNKS, NX, NZ, rows_out, LANES), STAGE_X), vmem((CHUNKS, NX, NZ, rows_out, LANES), STAGE_X),
        vmem((CHUNKS, NZ, rows_out, LANES), STAGE_Z), vmem((CHUNKS, NZ, rows_out, LANES), STAGE_Z),
        vmem((2, NY, 2, CHUNKS, rows_out, LANES), F32), vmem((ROWS, DIN), BF16), vmem((ROWS, 256), F32),
        vmem((DIN, LANES), F32),
        vmem((2, BLOCKS, LANES), F32), vmem((2, BLOCKS, LANES), F32), vmem((NX, BLOCKS, LANES), F32),
        vmem((NY, BLOCKS, LANES), F32), vmem((NZ, BLOCKS, LANES), F32), vmem((2, BLOCKS, LANES), F32),
        dma((4 + 3 * GROUPS,)), dma((2 + CHUNKS,)), dma((5,)), dma((5,)),
        dma((4,)), dma((3, 2)), dma((1,)), dma((1,)),
        dma((1,)), dma((1,)), dma((1,)), dma((2, 3, 2)), dma((2,)), dma((2,)), dma((4,)),
        dma((CHUNKS,)), dma((CHUNKS,)), dma((CHUNKS,)), dma((2, CHUNKS)),
        dma((CHUNKS,)), dma((CHUNKS,)), dma((CHUNKS,)), dma((CHUNKS,)), dma((CHUNKS,)), dma((CHUNKS,)), dma((1,)), dma((CHUNKS,)),
    ]
    grad_input, pieces, sums = pl.pallas_call(
        body,
        out_shape=(
            jax.ShapeDtypeStruct((ROWS, DIN), BF16),
            jax.ShapeDtypeStruct((2, NY, 2, CHUNKS, rows_out, LANES), F32),
            jax.ShapeDtypeStruct((2, BLOCKS, LANES), F32),
        ),
        in_specs=[any_space] * 7,
        out_specs=(any_space,) * 3,
        scratch_shapes=scratch,
        compiler_params=pltpu.CompilerParams(
            collective_id=0, has_side_effects=True, vmem_limit_bytes=56 * 1024 * 1024,
        ),
    )(
        features, normed, relu_mask, cotangent, weight_shard.reshape(2, 32, DOUT),
        norm_gain.reshape(BLOCKS, LANES), inverse_deviation.reshape(BLOCKS, LANES),
    )
    rescale = 1.0 / math.sqrt(ROWS * NZ * NX * NY * 2)
    grad_input, grad_weight, grad_gain, grad_shift = pl.pallas_call(
        functools.partial(finish, rescale),
        out_shape=(
            jax.ShapeDtypeStruct((ROWS, DIN), BF16),
            jax.ShapeDtypeStruct((2 * rows_out, DOUT), F32),
            jax.ShapeDtypeStruct((BLOCKS, LANES), F32),
            jax.ShapeDtypeStruct((BLOCKS, LANES), F32),
        ),
    )(grad_input, pieces.reshape(2, BLOCKS, rows_out, LANES), sums)
    return grad_input, grad_weight, grad_gain.reshape(DOUT), grad_shift.reshape(DOUT)


def solution(mesh):
    split = Mesh(mesh.devices.reshape(NZ, 2, NY, 2, 2), (Z, XH, Y, XL, C))
    rows = P((Z, XH, Y, XL, C), None)
    shard = P((Z, XH), None)
    return jax.shard_map(
        on_device,
        mesh=split,
        in_specs=(rows, rows, rows, rows, shard, P(), P()),
        out_specs=(rows, shard, P(), P()),
        check_vma=False,
    )
```

```python
import functools
import math

import jax
import jax.numpy as jnp
from jax import lax
from jax.experimental import pallas as pl
from jax.experimental.pallas import tpu as pltpu
from jax.sharding import Mesh
from jax.sharding import PartitionSpec as P

Z, XH, Y, XL, C = "z", "xh", "y", "xl", "c"
NZ, NX, NY = 8, 4, 4
F32, BF16 = jnp.float32, jnp.bfloat16

ROWS = 256
DIN = 1024
DOUT = 4096
LANES = 128
BLOCKS = DOUT // LANES
CHUNKS = BLOCKS // (NY * 2)
HALF = BLOCKS // 2
GROUPS = 4

STAGE_X = BF16
STAGE_Z = BF16


def body(
    feat_hbm, normed_hbm, mask_hbm, cot_hbm, w_hbm, gain_hbm, inv_hbm,
    gi_hbm, gw_hbm, stat_hbm,
    feat, normed, mask, cot, scale_a, scale_b, msk, wf, ft, ngs, ngr, rel,
    xs, xr, zs, zr, gw, gi, acc, near, st, st_core, st_x, st_y, st_z, st_all,
    load_sem, out_sem, stat_s, stat_r,
    f_s, f_r, fp_s, fp_r,
    wo_s, wo_r, wz_s, wz_r, wl_r, wp_s, wp_r,
    ng_s, near_r, far_r, rel_r,
    x_s, x_r, z_s, z_r, g_s, g_r, gp_s, gp_r,
):
    z, xh, y, xl, c = (lax.axis_index(name) for name in (Z, XH, Y, XL, C))
    x = 2 * xh + xl
    oc, oxh, oxl = 1 - c, 1 - xh, 1 - xl
    yp, ym, y2 = (y + 1) % NY, (y + 3) % NY, (y + 2) % NY
    zp, zm = (z + 1) % NZ, (z + NZ - 1) % NZ
    me = 2 * y + c
    partner = {C: oc}
    x_peers = [(oxh, xl), (oxh, oxl), (xh, oxl)]

    def remote(src, dst, ss, rs, device):
        return pltpu.make_async_remote_copy(
            src_ref=src, dst_ref=dst, send_sem=ss, recv_sem=rs,
            device_id=device, device_id_type=pl.DeviceIdType.MESH,
        )

    def send(src, dst, ss, rs, device):
        remote(src, dst, ss, rs, device).start()

    def arrived(ref, rs):
        remote(ref, ref, rs, rs, partner).wait_recv()

    def left(ref, ss):
        remote(ref, ref, ss, ss, partner).wait_send()

    load_feat = pltpu.make_async_copy(feat_hbm, feat, load_sem.at[0])
    load_w = pltpu.make_async_copy(w_hbm, wf.at[z, xh], load_sem.at[1])
    load_a = pltpu.make_async_copy(gain_hbm, scale_a, load_sem.at[2])
    load_b = pltpu.make_async_copy(inv_hbm, scale_b, load_sem.at[3])
    loads = []
    width = DOUT // GROUPS
    load_feat.start()
    load_w.start()
    for group in range(GROUPS):
        cols = pl.ds(group * width, width)
        loads.append([
            pltpu.make_async_copy(src.at[:, cols], dst.at[:, cols], load_sem.at[4 + 3 * group + k])
            for k, (src, dst) in enumerate(((cot_hbm, cot), (mask_hbm, mask), (normed_hbm, normed)))
        ])
        for copy in loads[-1]:
            copy.start()
    load_a.start()
    load_b.start()

    barrier = pltpu.get_barrier_semaphore()
    friends = [partner]
    for other in (yp, ym, y2):
        friends += [{Y: other, C: c}, {Y: other, C: oc}, {Y: other, XL: oxl}]
    friends += [{XH: a, XL: b} for a, b in x_peers]
    friends += [{Z: (z + k) % NZ} for k in range(1, NZ)]
    for friend in friends:
        pl.semaphore_signal(barrier, inc=1, device_id=friend, device_id_type=pl.DeviceIdType.MESH)

    load_feat.wait()
    for k in range(DIN // LANES):
        part = feat[:, k * LANES:(k + 1) * LANES]
        ft[me, k * LANES:(k + 1) * LANES, :] = part.T

    pl.semaphore_wait(barrier, len(friends))

    quarter = DIN // 4

    def feature(direction, q, late):
        ref = ft.at[me, pl.ds(q * quarter, quarter)]
        send(ref, ref, f_s.at[direction], f_r.at[late, direction], {Y: yp if direction == 0 else ym})

    feature(0, 0, 0)
    feature(1, 2, 0)
    def side(o):
        return xh if o == 0 else oxh

    def weights_on(direction, block, step, o):
        ref = wf.at[block, side(o), c]
        send(ref, ref, wz_s.at[0], wz_r.at[direction, step - 1, o], {Z: zp if direction == 0 else zm})

    def weights_next(step, o, start=True):
        blocks = [(z + NZ - step) % NZ, (z + step) % NZ]
        for direction, b in enumerate(blocks):
            if start:
                arrived(wf.at[b, side(o), c], wz_r.at[direction, step - 1, o])
            if step < 3:
                weights_on(direction, b, step + 1, o)
        if step == 3:
            for direction, b in enumerate(blocks):
                ref = wf.at[b, side(o), c, pl.ds(direction * 16, 16)]
                send(ref, ref, wz_s.at[0], wl_r.at[o], {Z: zp if direction == 0 else zm})
        for b in blocks:
            ref = wf.at[b, side(o), c]
            send(ref, ref, wp_s.at[0], wp_r.at[step - 1], partner)

    def weights_over():
        outer = {XH: oxh, XL: oxl}
        for direction, b in enumerate(((z + NZ - 1) % NZ, (z + 1) % NZ)):
            ref = wf.at[b, xh, c]
            arrived(ref, wz_r.at[direction, 0, 0])
            send(ref, ref, wo_s.at[0], wz_r.at[direction, 0, 1], outer)
        send(wf.at[z, xh, c], wf.at[z, xh, c], wo_s.at[0], wo_r.at[0], outer)

    def weights_last(o):
        ref = wf.at[(z + 4) % NZ, side(o), c]
        arrived(ref, wl_r.at[o])
        send(ref, ref, wp_s.at[0], wp_r.at[3], partner)

    load_w.wait()
    weights_on(0, z, 1, 0)
    weights_on(1, z, 1, 0)

    per_group = BLOCKS // GROUPS
    for group in range(GROUPS):
        for copy in loads[group]:
            copy.wait()

        def sums(i, carry):
            b = group * per_group + i
            cols = pl.ds(pl.multiple_of(b * LANES, LANES), LANES)
            value = jnp.where(mask[:, cols] != 0, cot[:, cols].astype(F32), 0.0)
            msk[b] = value.astype(BF16)
            half, row = b // HALF, b % HALF
            st[half, pl.ds(row, 1), :] = jnp.sum(value, axis=0, keepdims=True)
            cross = value * normed[:, cols].astype(F32)
            st[half, pl.ds(HALF + row, 1), :] = jnp.sum(cross, axis=0, keepdims=True)
            return carry

        lax.fori_loop(0, per_group, sums, 0)

    send(st.at[oc], st_core.at[c], stat_s.at[0], stat_r.at[0], partner)
    arrived(st_core.at[oc], stat_r.at[0])
    st_y[y] = st[c] + st_core[oc]
    for k in (2, 1, 3):
        send(st_y.at[y], st_y.at[y], stat_s.at[1], stat_r.at[1], {Y: (y + k) % NY})
    feature(0, 1, 0)
    feature(1, 3, 0)
    for late in ((2, 1), (3, 0)):
        for direction in range(2):
            feature(direction, late[direction], 1)
    arrived(st_y.at[pl.ds(0, NY - 1)], stat_r.at[1])
    st_x[x] = st_y[0] + st_y[1] + st_y[2] + st_y[3]
    for a, b in x_peers:
        send(st_x.at[x], st_x.at[x], stat_s.at[2], stat_r.at[2], {XH: a, XL: b})
    weights_over()
    arrived(st_x.at[pl.ds(0, NX - 1)], stat_r.at[2])
    st_z[z] = st_x[0] + st_x[1] + st_x[2] + st_x[3]
    for k in (4, 3, 5, 2, 6, 1, 7):
        send(st_z.at[z], st_z.at[z], stat_s.at[3], stat_r.at[3], {Z: (z + k) % NZ})
    mid = DIN // 2
    low, high = ft.at[2 * ym + c, pl.ds(0, mid)], ft.at[2 * yp + c, pl.ds(mid, mid)]
    arrived(low, f_r.at[0, 0])
    send(low, low, f_s.at[2], f_r.at[2, 0], {Y: yp})
    arrived(high, f_r.at[0, 1])
    send(high, high, f_s.at[3], f_r.at[2, 1], {Y: ym})
    weights_next(1, 0, start=False)
    arrived(st_z.at[pl.ds(0, NZ - 1)], stat_r.at[3])
    st_all[c] = sum((st_z[k] for k in range(1, NZ)), st_z[0])
    send(st_all.at[c], st_all.at[c], stat_s.at[4], stat_r.at[4], partner)
    send(ft.at[me], ft.at[me], fp_s.at[0], fp_r.at[0], partner)
    load_a.wait()
    load_b.wait()
    arrived(st_all.at[oc], stat_r.at[4])
    store_stat = pltpu.make_async_copy(st_all, stat_hbm, out_sem.at[0])
    store_stat.start()

    inverse_rows = 1.0 / (ROWS * NZ * NX * NY * 2)

    def norm_grad(j):
        def one(i, carry):
            b = i * CHUNKS + j
            cols = pl.ds(pl.multiple_of(b * LANES, LANES), LANES)
            half, row = b // HALF, b % HALF
            plain = st_all[half, pl.ds(row, 1), :] * inverse_rows
            cross = st_all[half, pl.ds(HALF + row, 1), :] * inverse_rows
            scale = scale_b[pl.ds(b, 1), :] * scale_a[pl.ds(b, 1), :]
            value = msk[b].astype(F32) - plain - normed[:, cols].astype(F32) * cross
            ngs[b] = (scale * value).astype(BF16)
            return carry

        lax.fori_loop(0, NY * 2, one, 0)
        ngr[j, me] = ngs[me * CHUNKS + j]

    def block(chip, core, j):
        return ngs.at[(chip * 2 + core) * CHUNKS + j]

    def send_far(j):
        send(block(y2, 0, j), rel.at[0, j], ng_s.at[j], rel_r.at[0, j], {Y: yp})
        send(block(y2, 1, j), rel.at[1, j], ng_s.at[j], rel_r.at[1, j], {Y: ym})

    def send_near(j):
        for core in range(2):
            for chip in (yp, ym):
                send(block(chip, core, j), ngr.at[j, me], ng_s.at[j], near_r.at[j], {Y: chip, C: core})
        send(block(y, oc, j), ngr.at[j, me], ng_s.at[j], near_r.at[j], partner)

    def pass_on(j):
        arrived(rel.at[0, j], rel_r.at[0, j])
        send(rel.at[0, j], ngr.at[j, 2 * ym + c], ng_s.at[j], far_r.at[j], {Y: yp, C: 0})
        arrived(rel.at[1, j], rel_r.at[1, j])
        send(rel.at[1, j], ngr.at[j, 2 * yp + c], ng_s.at[j], far_r.at[j], {Y: ym, C: 1})

    tall = 256

    def product(j, rows, sources):
        a = jnp.concatenate([ft[s, rows, :] for s in sources], axis=1)
        b = jnp.concatenate([ngr[j, s] for s in sources], axis=0)
        return jnp.dot(a, b, preferred_element_type=F32)

    def multiply_near(j):
        arrived(ngr.at[j, pl.ds(0, 5)], near_r.at[j])

        def tile(i, carry):
            rows = pl.ds(pl.multiple_of(i * tall, tall), tall)
            near[rows, :] = product(j, rows, [2 * chip + core for chip in (y, yp, ym) for core in range(2)])
            return carry

        lax.fori_loop(0, DIN // tall, tile, 0)

    def multiply_far(j):
        arrived(ngr.at[j, pl.ds(0, 2)], far_r.at[j])

        def tile(i, carry):
            rows = pl.ds(pl.multiple_of(i * tall, tall), tall)
            out = (near[rows, :] + product(j, rows, [2 * y2, 2 * y2 + 1])).astype(STAGE_X)
            each = DIN // NZ
            share = each // NX
            for a in range(tall // each):
                for b in range(NX):
                    xs[j, b, i * (tall // each) + a] = out[a * each + b * share:a * each + (b + 1) * share]
            ready = pl.ds(i * (tall // each), tall // each)
            for a, b in x_peers:
                send(xs.at[j, 2 * a + b, ready], xr.at[j, x, ready], x_s.at[j], x_r.at[j], {XH: a, XL: b})
            return carry

        lax.fori_loop(0, DIN // tall, tile, 0)
        xr[j, x] = xs[j, x]

    def over_x(j):
        arrived(xr.at[j, pl.ds(0, NX - 1)], x_r.at[j])
        total = xr[j, 0].astype(F32)
        for k in range(1, NX):
            total += xr[j, k].astype(F32)
        zs[j] = total.astype(STAGE_Z)
        for k in (4, 3, 5, 2, 6, 1, 7):
            to = (z + k) % NZ
            send(zs.at[j, to], zr.at[j, z], z_s.at[j], z_r.at[j], {Z: to})
        zr[j, z] = zs[j, z]

    others = [(chip, lane) for chip in (y2, yp, ym) for lane in (oxl, xl)] + [(y, oxl)]

    def over_z(j):
        arrived(zr.at[j, pl.ds(0, NZ - 1)], z_r.at[j])
        total = zr[j, 0].astype(F32)
        for k in range(1, NZ):
            total += zr[j, k].astype(F32)
        gw[xl, y, c, j] = total
        mine = gw.at[xl, y, c, j]
        for chip, lane in others:
            send(mine, mine, g_s.at[j], g_r.at[j], {Y: chip, XL: lane})

    def gathered(j):
        arrived(near.at[pl.ds(0, len(others) * 32)], g_r.at[j])
        part = gw.at[:, :, c, j]
        send(part, part, gp_s.at[0], gp_r.at[j], partner)

    def grad_input(step):
        if step == 4:
            arrived(wf.at[pl.ds(0, 3), 0, 0], wp_r.at[3])
            blocks = (z, (z + 4) % NZ)
        else:
            arrived(wf.at[pl.ds(0, 2), :, 0], wp_r.at[step - 1])
            blocks = ((z - step + NZ) % NZ, (z + step) % NZ)
        acc[...] = jnp.zeros_like(acc)
        deep = 1024

        def part(i, carry):
            cols = pl.ds(pl.multiple_of(i * deep, deep), deep)
            count = deep // LANES
            a = jnp.concatenate([ngs[i * count + k] for k in range(count)], axis=1)
            b = jnp.concatenate([wf[k, :, :, :, cols].reshape(LANES, deep) for k in blocks], axis=0)
            acc[...] += lax.dot_general(a, b, (((1,), (1,)), ((), ())), preferred_element_type=F32)
            return carry

        lax.fori_loop(0, DOUT // deep, part, 0)
        for k, place in enumerate(blocks):
            cols = pl.ds(pl.multiple_of(place * LANES, LANES), LANES)
            gi[:, cols] = acc[:, k * LANES:(k + 1) * LANES].astype(BF16)

    def store(j):
        arrived(gw.at[:, :, oc, j], gp_r.at[j])
        copy = pltpu.make_async_copy(gw.at[:, :, :, j], gw_hbm.at[:, :, :, j], out_sem.at[2 + j])
        copy.start()
        return copy

    norm_grad(0)
    send_far(0)
    send_near(0)
    norm_grad(1)
    send_far(1)
    norm_grad(2)
    norm_grad(3)
    arrived(ft.at[2 * ym + c, pl.ds(0, mid)], f_r.at[1, 0])
    arrived(ft.at[2 * yp + c, pl.ds(0, mid)], f_r.at[1, 1])
    for chip in (ym, yp):
        send(ft.at[2 * chip + c], ft.at[2 * chip + c], fp_s.at[0], fp_r.at[0], partner)
    pass_on(0)
    send_far(2)
    send_near(1)
    weights_next(1, 1)
    weights_next(2, 0)
    for direction in range(2):
        arrived(ft.at[2 * y2 + c, pl.ds(direction * mid, mid)], f_r.at[2, direction])
    send(ft.at[2 * y2 + c], ft.at[2 * y2 + c], fp_s.at[0], fp_r.at[0], partner)
    pass_on(1)
    send_far(3)
    send_near(2)
    far_out = wf.at[z, oxh, c]
    arrived(far_out, wo_r.at[0])
    send(far_out, far_out, wp_s.at[1], wp_r.at[3], partner)
    arrived(ft.at[pl.ds(0, 4)], fp_r.at[0])
    multiply_near(0)
    multiply_far(0)
    pass_on(2)
    send_near(3)
    multiply_near(1)
    weights_next(2, 1)
    multiply_far(1)
    pass_on(3)
    over_x(0)
    grad_input(1)
    weights_next(3, 0)
    multiply_near(2)
    multiply_far(2)
    over_x(1)
    grad_input(2)
    weights_next(3, 1)
    multiply_near(3)
    multiply_far(3)
    over_z(0)
    over_x(2)
    grad_input(3)
    weights_last(0)
    over_z(1)
    over_x(3)
    weights_last(1)
    over_z(2)
    gathered(0)
    grad_input(4)
    store_gi = pltpu.make_async_copy(gi, gi_hbm, out_sem.at[1])
    store_gi.start()
    over_z(3)
    gathered(1)
    gathered(2)
    stores = [store(j) for j in range(CHUNKS - 1)]
    gathered(3)
    stores.append(store(CHUNKS - 1))

    left(st.at[0], stat_s.at[0])
    left(st_y.at[pl.ds(0, NY - 1)], stat_s.at[1])
    left(st_x.at[pl.ds(0, NX - 1)], stat_s.at[2])
    left(st_z.at[pl.ds(0, NZ - 1)], stat_s.at[3])
    left(st.at[0], stat_s.at[4])
    for direction in range(2):
        left(ft.at[0], f_s.at[direction])
        left(low, f_s.at[2 + direction])
    left(ft.at[pl.ds(0, 4)], fp_s.at[0])
    left(wf.at[pl.ds(0, 3), 0, 0], wo_s.at[0])
    left(wf.at[pl.ds(0, 6), :, 0], wz_s.at[0])
    left(wf.at[pl.ds(0, 7), :, 0], wp_s.at[0])
    left(far_out, wp_s.at[1])
    for j in range(CHUNKS):
        left(ngs.at[pl.ds(0, 9)], ng_s.at[j])
        left(xr.at[j, pl.ds(0, NX - 1)], x_s.at[j])
        left(zr.at[j, pl.ds(0, NZ - 1)], z_s.at[j])
        left(near.at[pl.ds(0, len(others) * 32)], g_s.at[j])
    left(gw.at[:, :, c], gp_s.at[0])
    store_stat.wait()
    store_gi.wait()
    for copy in stores:
        copy.wait()


def finish(rescale, gi, gw, stat, gi_out, gw_out, gain_out, shift_out, gi_v, gw_v, stat_v, full, gain, shift, sems):
    parts = gw_v.shape[0]
    count = BLOCKS // (parts // 2)
    tall = gw.shape[2]

    def source(k):
        return gw.at[k // 2, pl.ds(k % 2 * count, count)]

    def target(k):
        return gw_out.at[pl.ds(k // 2 * tall, tall), pl.ds(k % 2 * count * LANES, count * LANES)]

    loads = [pltpu.make_async_copy(source(k), gw_v.at[k], sems.at[k]) for k in range(parts)]
    loads.append(pltpu.make_async_copy(gi, gi_v, sems.at[parts]))
    loads.append(pltpu.make_async_copy(stat, stat_v, sems.at[parts + 1]))
    for copy in loads:
        copy.start()
    stores = []

    def put(src, dst, sem):
        stores.append(pltpu.make_async_copy(src, dst, sem))
        stores[-1].start()

    for k in range(parts):
        loads[k].wait()
        for b in range(count):
            full[k, :, b * LANES:(b + 1) * LANES] = gw_v[k, b] * rescale
        put(full.at[k], target(k), sems.at[parts + 2 + k])
    loads[parts].wait()
    put(gi_v, gi_out, sems.at[2 * parts + 2])
    loads[parts + 1].wait()
    for half in range(2):
        rows = slice(half * HALF, (half + 1) * HALF)
        shift[rows, :] = stat_v[half, :HALF] * rescale
        gain[rows, :] = stat_v[half, HALF:] * rescale
    put(gain, gain_out, sems.at[2 * parts + 3])
    put(shift, shift_out, sems.at[2 * parts + 4])
    for copy in stores:
        copy.wait()


def on_device(features, normed, relu_mask, cotangent, weight_shard, norm_gain, inverse_deviation):
    dma = pltpu.SemaphoreType.DMA
    vmem = pltpu.VMEM
    any_space = pl.BlockSpec(memory_space=pl.ANY)
    rows_out = DIN // (NZ * NX)
    scratch = [
        vmem((ROWS, DIN), BF16), vmem((ROWS, DOUT), BF16), vmem((ROWS, DOUT), jnp.int32), vmem((ROWS, DOUT), BF16),
        vmem((BLOCKS, LANES), F32), vmem((BLOCKS, LANES), F32), vmem((BLOCKS, ROWS, LANES), BF16),
        vmem((NZ, 2, 2, 32, DOUT), BF16), vmem((NY * 2, DIN, ROWS), BF16),
        vmem((BLOCKS, ROWS, LANES), BF16), vmem((CHUNKS, NY * 2, ROWS, LANES), BF16), vmem((2, CHUNKS, ROWS, LANES), BF16),
        vmem((CHUNKS, NX, NZ, rows_out, LANES), STAGE_X), vmem((CHUNKS, NX, NZ, rows_out, LANES), STAGE_X),
        vmem((CHUNKS, NZ, rows_out, LANES), STAGE_Z), vmem((CHUNKS, NZ, rows_out, LANES), STAGE_Z),
        vmem((2, NY, 2, CHUNKS, rows_out, LANES), F32), vmem((ROWS, DIN), BF16), vmem((ROWS, 256), F32),
        vmem((DIN, LANES), F32),
        vmem((2, BLOCKS, LANES), F32), vmem((2, BLOCKS, LANES), F32), vmem((NX, BLOCKS, LANES), F32),
        vmem((NY, BLOCKS, LANES), F32), vmem((NZ, BLOCKS, LANES), F32), vmem((2, BLOCKS, LANES), F32),
        dma((4 + 3 * GROUPS,)), dma((2 + CHUNKS,)), dma((5,)), dma((5,)),
        dma((4,)), dma((3, 2)), dma((1,)), dma((1,)),
        dma((1,)), dma((1,)), dma((1,)), dma((2, 3, 2)), dma((2,)), dma((2,)), dma((4,)),
        dma((CHUNKS,)), dma((CHUNKS,)), dma((CHUNKS,)), dma((2, CHUNKS)),
        dma((CHUNKS,)), dma((CHUNKS,)), dma((CHUNKS,)), dma((CHUNKS,)), dma((CHUNKS,)), dma((CHUNKS,)), dma((1,)), dma((CHUNKS,)),
    ]
    grad_input, pieces, sums = pl.pallas_call(
        body,
        out_shape=(
            jax.ShapeDtypeStruct((ROWS, DIN), BF16),
            jax.ShapeDtypeStruct((2, NY, 2, CHUNKS, rows_out, LANES), F32),
            jax.ShapeDtypeStruct((2, BLOCKS, LANES), F32),
        ),
        in_specs=[any_space] * 7,
        out_specs=(any_space,) * 3,
        scratch_shapes=scratch,
        compiler_params=pltpu.CompilerParams(
            collective_id=0, has_side_effects=True, vmem_limit_bytes=56 * 1024 * 1024,
        ),
    )(
        features, normed, relu_mask, cotangent, weight_shard.reshape(2, 32, DOUT),
        norm_gain.reshape(BLOCKS, LANES), inverse_deviation.reshape(BLOCKS, LANES),
    )
    steps = 4
    rescale = 1.0 / math.sqrt(ROWS * NZ * NX * NY * 2)
    grad_input, grad_weight, grad_gain, grad_shift = pl.pallas_call(
        functools.partial(finish, rescale),
        out_shape=(
            jax.ShapeDtypeStruct((ROWS, DIN), BF16),
            jax.ShapeDtypeStruct((2 * rows_out, DOUT), F32),
            jax.ShapeDtypeStruct((BLOCKS, LANES), F32),
            jax.ShapeDtypeStruct((BLOCKS, LANES), F32),
        ),
        in_specs=[any_space] * 3,
        out_specs=(any_space,) * 4,
        scratch_shapes=[
            vmem((ROWS, DIN), BF16), vmem((steps, 2 * BLOCKS // steps, rows_out, LANES), F32), vmem((2, BLOCKS, LANES), F32),
            vmem((steps, rows_out, DOUT * 2 // steps), F32), vmem((BLOCKS, LANES), F32), vmem((BLOCKS, LANES), F32),
            dma((2 * steps + 5,)),
        ],
    )(grad_input, pieces.reshape(2, BLOCKS, rows_out, LANES), sums)
    return grad_input, grad_weight, grad_gain.reshape(DOUT), grad_shift.reshape(DOUT)


def solution(mesh):
    split = Mesh(mesh.devices.reshape(NZ, 2, NY, 2, 2), (Z, XH, Y, XL, C))
    rows = P((Z, XH, Y, XL, C), None)
    shard = P((Z, XH), None)
    return jax.shard_map(
        on_device,
        mesh=split,
        in_specs=(rows, rows, rows, rows, shard, P(), P()),
        out_specs=(rows, shard, P(), P()),
        check_vma=False,
    )
```

```python
import functools
import math

import jax
import jax.numpy as jnp
from jax import lax
from jax.experimental import pallas as pl
from jax.experimental.pallas import tpu as pltpu
from jax.sharding import Mesh
from jax.sharding import PartitionSpec as P

Z, XH, Y, XL, C = "z", "xh", "y", "xl", "c"
NZ, NX, NY = 8, 4, 4
F32, BF16 = jnp.float32, jnp.bfloat16

ROWS = 256
DIN = 1024
DOUT = 4096
LANES = 128
BLOCKS = DOUT // LANES
CHUNKS = BLOCKS // (NY * 2)
HALF = BLOCKS // 2
GROUPS = 4

STAGE_X = BF16
STAGE_Z = BF16


def body(
    feat_hbm, normed_hbm, mask_hbm, cot_hbm, w_hbm, gain_hbm, inv_hbm,
    gi_hbm, gw_hbm, stat_hbm,
    feat, normed, mask, cot, scale_a, scale_b, msk, wf, ft, ngs, ngr, rel,
    xs, xr, zs, zr, gw, gi, acc, near, st, st_core, st_x, st_y, st_z, st_all,
    load_sem, out_sem, stat_s, stat_r,
    f_s, f_r, fp_s, fp_r,
    wo_s, wo_r, wz_s, wz_r, wl_r, wp_s, wp_r,
    ng_s, near_r, far_r, rel_r,
    x_s, x_r, z_s, z_r, g_s, g_r, gp_s, gp_r,
):
    z, xh, y, xl, c = (lax.axis_index(name) for name in (Z, XH, Y, XL, C))
    x = 2 * xh + xl
    oc, oxh, oxl = 1 - c, 1 - xh, 1 - xl
    yp, ym, y2 = (y + 1) % NY, (y + 3) % NY, (y + 2) % NY
    zp, zm = (z + 1) % NZ, (z + NZ - 1) % NZ
    me = 2 * y + c
    partner = {C: oc}
    x_peers = [(oxh, xl), (oxh, oxl), (xh, oxl)]

    def remote(src, dst, ss, rs, device):
        return pltpu.make_async_remote_copy(
            src_ref=src, dst_ref=dst, send_sem=ss, recv_sem=rs,
            device_id=device, device_id_type=pl.DeviceIdType.MESH,
        )

    def send(src, dst, ss, rs, device):
        remote(src, dst, ss, rs, device).start()

    def arrived(ref, rs):
        remote(ref, ref, rs, rs, partner).wait_recv()

    def left(ref, ss):
        remote(ref, ref, ss, ss, partner).wait_send()

    load_feat = pltpu.make_async_copy(feat_hbm, feat, load_sem.at[0])
    load_w = pltpu.make_async_copy(w_hbm, wf.at[z, xh], load_sem.at[1])
    load_a = pltpu.make_async_copy(gain_hbm, scale_a, load_sem.at[2])
    load_b = pltpu.make_async_copy(inv_hbm, scale_b, load_sem.at[3])
    loads = []
    width = DOUT // GROUPS
    load_feat.start()
    load_w.start()
    for group in range(GROUPS):
        cols = pl.ds(group * width, width)
        loads.append([
            pltpu.make_async_copy(src.at[:, cols], dst.at[:, cols], load_sem.at[4 + 3 * group + k])
            for k, (src, dst) in enumerate(((cot_hbm, cot), (mask_hbm, mask), (normed_hbm, normed)))
        ])
        for copy in loads[-1]:
            copy.start()
    load_a.start()
    load_b.start()

    barrier = pltpu.get_barrier_semaphore()
    friends = [partner]
    for other in (yp, ym, y2):
        friends += [{Y: other, C: c}, {Y: other, C: oc}, {Y: other, XL: oxl}]
    friends += [{XH: a, XL: b} for a, b in x_peers]
    friends += [{Z: (z + k) % NZ} for k in range(1, NZ)]
    for friend in friends:
        pl.semaphore_signal(barrier, inc=1, device_id=friend, device_id_type=pl.DeviceIdType.MESH)

    load_feat.wait()
    for k in range(DIN // LANES):
        part = feat[:, k * LANES:(k + 1) * LANES]
        ft[me, k * LANES:(k + 1) * LANES, :] = part.T

    pl.semaphore_wait(barrier, len(friends))

    quarter = DIN // 4

    def feature(direction, q, late):
        ref = ft.at[me, pl.ds(q * quarter, quarter)]
        send(ref, ref, f_s.at[direction], f_r.at[late, direction], {Y: yp if direction == 0 else ym})

    feature(0, 0, 0)
    feature(1, 2, 0)
    def side(o):
        return xh if o == 0 else oxh

    def weights_on(direction, block, step, o):
        ref = wf.at[block, side(o), c]
        send(ref, ref, wz_s.at[0], wz_r.at[direction, step - 1, o], {Z: zp if direction == 0 else zm})

    def weights_next(step, o, start=True):
        blocks = [(z + NZ - step) % NZ, (z + step) % NZ]
        for direction, b in enumerate(blocks):
            if start:
                arrived(wf.at[b, side(o), c], wz_r.at[direction, step - 1, o])
            if step < 3:
                weights_on(direction, b, step + 1, o)
        if step == 3:
            for direction, b in enumerate(blocks):
                ref = wf.at[b, side(o), c, pl.ds(direction * 16, 16)]
                send(ref, ref, wz_s.at[0], wl_r.at[o], {Z: zp if direction == 0 else zm})
        for b in blocks:
            ref = wf.at[b, side(o), c]
            send(ref, ref, wp_s.at[0], wp_r.at[step - 1], partner)

    def weights_over():
        outer = {XH: oxh, XL: oxl}
        for direction, b in enumerate(((z + NZ - 1) % NZ, (z + 1) % NZ)):
            ref = wf.at[b, xh, c]
            arrived(ref, wz_r.at[direction, 0, 0])
            send(ref, ref, wo_s.at[0], wz_r.at[direction, 0, 1], outer)
        send(wf.at[z, xh, c], wf.at[z, xh, c], wo_s.at[0], wo_r.at[0], outer)

    def weights_last(o):
        ref = wf.at[(z + 4) % NZ, side(o), c]
        arrived(ref, wl_r.at[o])
        send(ref, ref, wp_s.at[0], wp_r.at[3], partner)

    load_w.wait()
    weights_on(0, z, 1, 0)
    weights_on(1, z, 1, 0)

    per_group = BLOCKS // GROUPS
    for group in range(GROUPS):
        for copy in loads[group]:
            copy.wait()

        def sums(i, carry):
            b = group * per_group + i
            cols = pl.ds(pl.multiple_of(b * LANES, LANES), LANES)
            value = jnp.where(mask[:, cols] != 0, cot[:, cols].astype(F32), 0.0)
            msk[b] = value.astype(BF16)
            half, row = b // HALF, b % HALF
            st[half, pl.ds(row, 1), :] = jnp.sum(value, axis=0, keepdims=True)
            cross = value * normed[:, cols].astype(F32)
            st[half, pl.ds(HALF + row, 1), :] = jnp.sum(cross, axis=0, keepdims=True)
            return carry

        lax.fori_loop(0, per_group, sums, 0)

    send(st.at[oc], st_core.at[c], stat_s.at[0], stat_r.at[0], partner)
    arrived(st_core.at[oc], stat_r.at[0])
    st_y[y] = st[c] + st_core[oc]
    for k in (2, 1, 3):
        send(st_y.at[y], st_y.at[y], stat_s.at[1], stat_r.at[1], {Y: (y + k) % NY})
    feature(0, 1, 0)
    feature(1, 3, 0)
    for late in ((2, 1), (3, 0)):
        for direction in range(2):
            feature(direction, late[direction], 1)
    arrived(st_y.at[pl.ds(0, NY - 1)], stat_r.at[1])
    st_x[x] = st_y[0] + st_y[1] + st_y[2] + st_y[3]
    for a, b in x_peers:
        send(st_x.at[x], st_x.at[x], stat_s.at[2], stat_r.at[2], {XH: a, XL: b})
    weights_over()
    arrived(st_x.at[pl.ds(0, NX - 1)], stat_r.at[2])
    st_z[z] = st_x[0] + st_x[1] + st_x[2] + st_x[3]
    for k in (4, 3, 5, 2, 6, 1, 7):
        send(st_z.at[z], st_z.at[z], stat_s.at[3], stat_r.at[3], {Z: (z + k) % NZ})
    mid = DIN // 2
    low, high = ft.at[2 * ym + c, pl.ds(0, mid)], ft.at[2 * yp + c, pl.ds(mid, mid)]
    arrived(low, f_r.at[0, 0])
    send(low, low, f_s.at[2], f_r.at[2, 0], {Y: yp})
    arrived(high, f_r.at[0, 1])
    send(high, high, f_s.at[3], f_r.at[2, 1], {Y: ym})
    weights_next(1, 0, start=False)
    arrived(st_z.at[pl.ds(0, NZ - 1)], stat_r.at[3])
    st_all[c] = sum((st_z[k] for k in range(1, NZ)), st_z[0])
    send(st_all.at[c], st_all.at[c], stat_s.at[4], stat_r.at[4], partner)
    send(ft.at[me], ft.at[me], fp_s.at[0], fp_r.at[0], partner)
    load_a.wait()
    load_b.wait()
    arrived(st_all.at[oc], stat_r.at[4])
    store_stat = pltpu.make_async_copy(st_all, stat_hbm, out_sem.at[0])
    store_stat.start()

    inverse_rows = 1.0 / (ROWS * NZ * NX * NY * 2)

    def norm_grad(j):
        def one(i, carry):
            b = i * CHUNKS + j
            cols = pl.ds(pl.multiple_of(b * LANES, LANES), LANES)
            half, row = b // HALF, b % HALF
            plain = st_all[half, pl.ds(row, 1), :] * inverse_rows
            cross = st_all[half, pl.ds(HALF + row, 1), :] * inverse_rows
            scale = scale_b[pl.ds(b, 1), :] * scale_a[pl.ds(b, 1), :]
            value = msk[b].astype(F32) - plain - normed[:, cols].astype(F32) * cross
            ngs[b] = (scale * value).astype(BF16)
            return carry

        lax.fori_loop(0, NY * 2, one, 0)
        ngr[j, me] = ngs[me * CHUNKS + j]

    def block(chip, core, j):
        return ngs.at[(chip * 2 + core) * CHUNKS + j]

    def send_far(j):
        send(block(y2, 0, j), rel.at[0, j], ng_s.at[j], rel_r.at[0, j], {Y: yp})
        send(block(y2, 1, j), rel.at[1, j], ng_s.at[j], rel_r.at[1, j], {Y: ym})

    def send_near_to(j, chip, core):
        send(block(chip, core, j), ngr.at[j, me], ng_s.at[j], near_r.at[j], {Y: chip, C: core})

    def send_near(j, cores=(0, 1)):
        for core in cores:
            for chip in (yp, ym):
                send_near_to(j, chip, core)
        send(block(y, oc, j), ngr.at[j, me], ng_s.at[j], near_r.at[j], partner)

    def pass_on(j, late=False):
        arrived(rel.at[0, j], rel_r.at[0, j])
        send(rel.at[0, j], ngr.at[j, 2 * ym + c], ng_s.at[j], far_r.at[j], {Y: yp, C: 0})
        if late:
            send_near_to(j, yp, 1)
            send_near_to(j, ym, 1)
        arrived(rel.at[1, j], rel_r.at[1, j])
        send(rel.at[1, j], ngr.at[j, 2 * yp + c], ng_s.at[j], far_r.at[j], {Y: ym, C: 1})

    tall = 256

    def product(j, rows, sources):
        a = jnp.concatenate([ft[s, rows, :] for s in sources], axis=1)
        b = jnp.concatenate([ngr[j, s] for s in sources], axis=0)
        return jnp.dot(a, b, preferred_element_type=F32)

    def multiply_near(j):
        arrived(ngr.at[j, pl.ds(0, 5)], near_r.at[j])

        def tile(i, carry):
            rows = pl.ds(pl.multiple_of(i * tall, tall), tall)
            near[rows, :] = product(j, rows, [2 * chip + core for chip in (y, yp, ym) for core in range(2)])
            return carry

        lax.fori_loop(0, DIN // tall, tile, 0)

    def multiply_far(j):
        arrived(ngr.at[j, pl.ds(0, 2)], far_r.at[j])

        def tile(i, carry):
            rows = pl.ds(pl.multiple_of(i * tall, tall), tall)
            out = (near[rows, :] + product(j, rows, [2 * y2, 2 * y2 + 1])).astype(STAGE_X)
            each = DIN // NZ
            share = each // NX
            for a in range(tall // each):
                for b in range(NX):
                    xs[j, b, i * (tall // each) + a] = out[a * each + b * share:a * each + (b + 1) * share]
            ready = pl.ds(i * (tall // each), tall // each)
            for a, b in x_peers:
                send(xs.at[j, 2 * a + b, ready], xr.at[j, x, ready], x_s.at[j], x_r.at[j], {XH: a, XL: b})
            return carry

        lax.fori_loop(0, DIN // tall, tile, 0)
        xr[j, x] = xs[j, x]

    def over_x(j):
        arrived(xr.at[j, pl.ds(0, NX - 1)], x_r.at[j])
        total = xr[j, 0].astype(F32)
        for k in range(1, NX):
            total += xr[j, k].astype(F32)
        zs[j] = total.astype(STAGE_Z)
        for k in (4, 3, 5, 2, 6, 1, 7):
            to = (z + k) % NZ
            send(zs.at[j, to], zr.at[j, z], z_s.at[j], z_r.at[j], {Z: to})
        zr[j, z] = zs[j, z]

    others = [(chip, lane) for chip in (y2, yp, ym) for lane in (oxl, xl)] + [(y, oxl)]

    def over_z(j):
        arrived(zr.at[j, pl.ds(0, NZ - 1)], z_r.at[j])
        total = zr[j, 0].astype(F32)
        for k in range(1, NZ):
            total += zr[j, k].astype(F32)
        gw[xl, y, c, j] = total
        mine = gw.at[xl, y, c, j]
        for chip, lane in others:
            send(mine, mine, g_s.at[j], g_r.at[j], {Y: chip, XL: lane})

    def gathered(j):
        arrived(near.at[pl.ds(0, len(others) * 32)], g_r.at[j])
        part = gw.at[:, :, c, j]
        send(part, part, gp_s.at[0], gp_r.at[j], partner)

    def grad_input(step):
        if step == 4:
            arrived(wf.at[pl.ds(0, 3), 0, 0], wp_r.at[3])
            blocks = (z, (z + 4) % NZ)
        else:
            arrived(wf.at[pl.ds(0, 2), :, 0], wp_r.at[step - 1])
            blocks = ((z - step + NZ) % NZ, (z + step) % NZ)
        acc[...] = jnp.zeros_like(acc)
        deep = 1024

        def part(i, carry):
            cols = pl.ds(pl.multiple_of(i * deep, deep), deep)
            count = deep // LANES
            a = jnp.concatenate([ngs[i * count + k] for k in range(count)], axis=1)
            b = jnp.concatenate([wf[k, :, :, :, cols].reshape(LANES, deep) for k in blocks], axis=0)
            acc[...] += lax.dot_general(a, b, (((1,), (1,)), ((), ())), preferred_element_type=F32)
            return carry

        lax.fori_loop(0, DOUT // deep, part, 0)
        for k, place in enumerate(blocks):
            cols = pl.ds(pl.multiple_of(place * LANES, LANES), LANES)
            gi[:, cols] = acc[:, k * LANES:(k + 1) * LANES].astype(BF16)

    def store(j):
        arrived(gw.at[:, :, oc, j], gp_r.at[j])
        copy = pltpu.make_async_copy(gw.at[:, :, :, j], gw_hbm.at[:, :, :, j], out_sem.at[2 + j])
        copy.start()
        return copy

    norm_grad(0)
    send_far(0)
    send_near(0)
    norm_grad(1)
    send_far(1)
    norm_grad(2)
    norm_grad(3)
    arrived(ft.at[2 * ym + c, pl.ds(0, mid)], f_r.at[1, 0])
    arrived(ft.at[2 * yp + c, pl.ds(0, mid)], f_r.at[1, 1])
    for chip in (ym, yp):
        send(ft.at[2 * chip + c], ft.at[2 * chip + c], fp_s.at[0], fp_r.at[0], partner)
    pass_on(0)
    send_far(2)
    send_near(1)
    weights_next(1, 1)
    weights_next(2, 0)
    for direction in range(2):
        arrived(ft.at[2 * y2 + c, pl.ds(direction * mid, mid)], f_r.at[2, direction])
    send(ft.at[2 * y2 + c], ft.at[2 * y2 + c], fp_s.at[0], fp_r.at[0], partner)
    pass_on(1)
    send_far(3)
    send_near(2)
    far_out = wf.at[z, oxh, c]
    arrived(far_out, wo_r.at[0])
    send(far_out, far_out, wp_s.at[1], wp_r.at[3], partner)
    arrived(ft.at[pl.ds(0, 4)], fp_r.at[0])
    multiply_near(0)
    multiply_far(0)
    send_near(3, (0,))
    pass_on(2)
    multiply_near(1)
    weights_next(2, 1)
    multiply_far(1)
    pass_on(3, late=True)
    over_x(0)
    grad_input(1)
    weights_next(3, 0)
    multiply_near(2)
    multiply_far(2)
    over_x(1)
    multiply_near(3)
    multiply_far(3)
    weights_next(3, 1)
    over_z(0)
    over_x(2)
    grad_input(2)
    weights_last(0)
    over_z(1)
    over_x(3)
    grad_input(3)
    over_z(2)
    weights_last(1)
    gathered(0)
    over_z(3)
    grad_input(4)
    store_gi = pltpu.make_async_copy(gi, gi_hbm, out_sem.at[1])
    store_gi.start()
    gathered(1)
    gathered(2)
    stores = [store(j) for j in range(CHUNKS - 1)]
    gathered(3)
    stores.append(store(CHUNKS - 1))

    left(st.at[0], stat_s.at[0])
    left(st_y.at[pl.ds(0, NY - 1)], stat_s.at[1])
    left(st_x.at[pl.ds(0, NX - 1)], stat_s.at[2])
    left(st_z.at[pl.ds(0, NZ - 1)], stat_s.at[3])
    left(st.at[0], stat_s.at[4])
    for direction in range(2):
        left(ft.at[0], f_s.at[direction])
        left(low, f_s.at[2 + direction])
    left(ft.at[pl.ds(0, 4)], fp_s.at[0])
    left(wf.at[pl.ds(0, 3), 0, 0], wo_s.at[0])
    left(wf.at[pl.ds(0, 6), :, 0], wz_s.at[0])
    left(wf.at[pl.ds(0, 7), :, 0], wp_s.at[0])
    left(far_out, wp_s.at[1])
    for j in range(CHUNKS):
        left(ngs.at[pl.ds(0, 9)], ng_s.at[j])
        left(xr.at[j, pl.ds(0, NX - 1)], x_s.at[j])
        left(zr.at[j, pl.ds(0, NZ - 1)], z_s.at[j])
        left(near.at[pl.ds(0, len(others) * 32)], g_s.at[j])
    left(gw.at[:, :, c], gp_s.at[0])
    store_stat.wait()
    store_gi.wait()
    for copy in stores:
        copy.wait()


def finish(rescale, gi, gw, stat, gi_out, gw_out, gain_out, shift_out, gi_v, gw_v, stat_v, full, gain, shift, sems):
    parts = gw_v.shape[0]
    count = BLOCKS // (parts // 2)
    tall = gw.shape[2]

    def source(k):
        return gw.at[k // 2, pl.ds(k % 2 * count, count)]

    def target(k):
        return gw_out.at[pl.ds(k // 2 * tall, tall), pl.ds(k % 2 * count * LANES, count * LANES)]

    loads = [pltpu.make_async_copy(source(k), gw_v.at[k], sems.at[k]) for k in range(parts)]
    loads.append(pltpu.make_async_copy(gi, gi_v, sems.at[parts]))
    loads.append(pltpu.make_async_copy(stat, stat_v, sems.at[parts + 1]))
    for copy in loads:
        copy.start()
    stores = []

    def put(src, dst, sem):
        stores.append(pltpu.make_async_copy(src, dst, sem))
        stores[-1].start()

    for k in range(parts):
        loads[k].wait()
        for b in range(count):
            full[k, :, b * LANES:(b + 1) * LANES] = gw_v[k, b] * rescale
        put(full.at[k], target(k), sems.at[parts + 2 + k])
    loads[parts].wait()
    put(gi_v, gi_out, sems.at[2 * parts + 2])
    loads[parts + 1].wait()
    for half in range(2):
        rows = slice(half * HALF, (half + 1) * HALF)
        shift[rows, :] = stat_v[half, :HALF] * rescale
        gain[rows, :] = stat_v[half, HALF:] * rescale
    put(gain, gain_out, sems.at[2 * parts + 3])
    put(shift, shift_out, sems.at[2 * parts + 4])
    for copy in stores:
        copy.wait()


def on_device(features, normed, relu_mask, cotangent, weight_shard, norm_gain, inverse_deviation):
    dma = pltpu.SemaphoreType.DMA
    vmem = pltpu.VMEM
    any_space = pl.BlockSpec(memory_space=pl.ANY)
    rows_out = DIN // (NZ * NX)
    scratch = [
        vmem((ROWS, DIN), BF16), vmem((ROWS, DOUT), BF16), vmem((ROWS, DOUT), jnp.int32), vmem((ROWS, DOUT), BF16),
        vmem((BLOCKS, LANES), F32), vmem((BLOCKS, LANES), F32), vmem((BLOCKS, ROWS, LANES), BF16),
        vmem((NZ, 2, 2, 32, DOUT), BF16), vmem((NY * 2, DIN, ROWS), BF16),
        vmem((BLOCKS, ROWS, LANES), BF16), vmem((CHUNKS, NY * 2, ROWS, LANES), BF16), vmem((2, CHUNKS, ROWS, LANES), BF16),
        vmem((CHUNKS, NX, NZ, rows_out, LANES), STAGE_X), vmem((CHUNKS, NX, NZ, rows_out, LANES), STAGE_X),
        vmem((CHUNKS, NZ, rows_out, LANES), STAGE_Z), vmem((CHUNKS, NZ, rows_out, LANES), STAGE_Z),
        vmem((2, NY, 2, CHUNKS, rows_out, LANES), F32), vmem((ROWS, DIN), BF16), vmem((ROWS, 256), F32),
        vmem((DIN, LANES), F32),
        vmem((2, BLOCKS, LANES), F32), vmem((2, BLOCKS, LANES), F32), vmem((NX, BLOCKS, LANES), F32),
        vmem((NY, BLOCKS, LANES), F32), vmem((NZ, BLOCKS, LANES), F32), vmem((2, BLOCKS, LANES), F32),
        dma((4 + 3 * GROUPS,)), dma((2 + CHUNKS,)), dma((5,)), dma((5,)),
        dma((4,)), dma((3, 2)), dma((1,)), dma((1,)),
        dma((1,)), dma((1,)), dma((1,)), dma((2, 3, 2)), dma((2,)), dma((2,)), dma((4,)),
        dma((CHUNKS,)), dma((CHUNKS,)), dma((CHUNKS,)), dma((2, CHUNKS)),
        dma((CHUNKS,)), dma((CHUNKS,)), dma((CHUNKS,)), dma((CHUNKS,)), dma((CHUNKS,)), dma((CHUNKS,)), dma((1,)), dma((CHUNKS,)),
    ]
    grad_input, pieces, sums = pl.pallas_call(
        body,
        out_shape=(
            jax.ShapeDtypeStruct((ROWS, DIN), BF16),
            jax.ShapeDtypeStruct((2, NY, 2, CHUNKS, rows_out, LANES), F32),
            jax.ShapeDtypeStruct((2, BLOCKS, LANES), F32),
        ),
        in_specs=[any_space] * 7,
        out_specs=(any_space,) * 3,
        scratch_shapes=scratch,
        compiler_params=pltpu.CompilerParams(
            collective_id=0, has_side_effects=True, vmem_limit_bytes=56 * 1024 * 1024,
        ),
    )(
        features, normed, relu_mask, cotangent, weight_shard.reshape(2, 32, DOUT),
        norm_gain.reshape(BLOCKS, LANES), inverse_deviation.reshape(BLOCKS, LANES),
    )
    steps = 4
    rescale = 1.0 / math.sqrt(ROWS * NZ * NX * NY * 2)
    grad_input, grad_weight, grad_gain, grad_shift = pl.pallas_call(
        functools.partial(finish, rescale),
        out_shape=(
            jax.ShapeDtypeStruct((ROWS, DIN), BF16),
            jax.ShapeDtypeStruct((2 * rows_out, DOUT), F32),
            jax.ShapeDtypeStruct((BLOCKS, LANES), F32),
            jax.ShapeDtypeStruct((BLOCKS, LANES), F32),
        ),
        in_specs=[any_space] * 3,
        out_specs=(any_space,) * 4,
        scratch_shapes=[
            vmem((ROWS, DIN), BF16), vmem((steps, 2 * BLOCKS // steps, rows_out, LANES), F32), vmem((2, BLOCKS, LANES), F32),
            vmem((steps, rows_out, DOUT * 2 // steps), F32), vmem((BLOCKS, LANES), F32), vmem((BLOCKS, LANES), F32),
            dma((2 * steps + 5,)),
        ],
    )(grad_input, pieces.reshape(2, BLOCKS, rows_out, LANES), sums)
    return grad_input, grad_weight, grad_gain.reshape(DOUT), grad_shift.reshape(DOUT)


def solution(mesh):
    split = Mesh(mesh.devices.reshape(NZ, 2, NY, 2, 2), (Z, XH, Y, XL, C))
    rows = P((Z, XH, Y, XL, C), None)
    shard = P((Z, XH), None)
    return jax.shard_map(
        on_device,
        mesh=split,
        in_specs=(rows, rows, rows, rows, shard, P(), P()),
        out_specs=(rows, shard, P(), P()),
        check_vma=False,
    )
```

```python
import functools
import math

import jax
import jax.numpy as jnp
from jax import lax
from jax.experimental import pallas as pl
from jax.experimental.pallas import tpu as pltpu
from jax.sharding import Mesh
from jax.sharding import PartitionSpec as P

Z, XH, Y, XL, C = "z", "xh", "y", "xl", "c"
NZ, NX, NY = 8, 4, 4
F32, BF16 = jnp.float32, jnp.bfloat16

ROWS = 256
DIN = 1024
DOUT = 4096
LANES = 128
BLOCKS = DOUT // LANES
CHUNKS = BLOCKS // (NY * 2)
HALF = BLOCKS // 2
GROUPS = 4

STAGE_X = BF16
STAGE_Z = BF16


def body(
    feat_hbm, normed_hbm, mask_hbm, cot_hbm, w_hbm, gain_hbm, inv_hbm,
    gi_hbm, gw_hbm, stat_hbm,
    feat, normed, mask, cot, scale_a, scale_b, msk, wf, ft, ngs, ngr, rel,
    xs, xr, zs, zr, gw, gi, acc, near, st, st_core, st_x, st_y, st_z, st_all,
    load_sem, out_sem, stat_s, stat_r,
    f_s, f_r, fp_s, fp_r,
    wo_s, wo_r, wz_s, wz_r, wl_r, wp_s, wp_r,
    ng_s, near_r, far_r, rel_r,
    x_s, x_r, z_s, z_r, g_s, g_r, gp_s, gp_r,
):
    z, xh, y, xl, c = (lax.axis_index(name) for name in (Z, XH, Y, XL, C))
    x = 2 * xh + xl
    oc, oxh, oxl = 1 - c, 1 - xh, 1 - xl
    yp, ym, y2 = (y + 1) % NY, (y + 3) % NY, (y + 2) % NY
    zp, zm = (z + 1) % NZ, (z + NZ - 1) % NZ
    me = 2 * y + c
    partner = {C: oc}
    x_peers = [(oxh, xl), (oxh, oxl), (xh, oxl)]

    def remote(src, dst, ss, rs, device):
        return pltpu.make_async_remote_copy(
            src_ref=src, dst_ref=dst, send_sem=ss, recv_sem=rs,
            device_id=device, device_id_type=pl.DeviceIdType.MESH,
        )

    def send(src, dst, ss, rs, device):
        remote(src, dst, ss, rs, device).start()

    def arrived(ref, rs):
        remote(ref, ref, rs, rs, partner).wait_recv()

    def left(ref, ss):
        remote(ref, ref, ss, ss, partner).wait_send()

    load_feat = pltpu.make_async_copy(feat_hbm, feat, load_sem.at[0])
    load_w = pltpu.make_async_copy(w_hbm, wf.at[z, xh], load_sem.at[1])
    load_a = pltpu.make_async_copy(gain_hbm, scale_a, load_sem.at[2])
    load_b = pltpu.make_async_copy(inv_hbm, scale_b, load_sem.at[3])
    loads = []
    width = DOUT // GROUPS
    load_feat.start()
    load_w.start()
    for group in range(GROUPS):
        cols = pl.ds(group * width, width)
        loads.append([
            pltpu.make_async_copy(src.at[:, cols], dst.at[:, cols], load_sem.at[4 + 3 * group + k])
            for k, (src, dst) in enumerate(((cot_hbm, cot), (mask_hbm, mask), (normed_hbm, normed)))
        ])
        for copy in loads[-1]:
            copy.start()
    load_a.start()
    load_b.start()

    barrier = pltpu.get_barrier_semaphore()
    friends = [partner]
    for other in (yp, ym, y2):
        friends += [{Y: other, C: c}, {Y: other, C: oc}, {Y: other, XL: oxl}]
    friends += [{XH: a, XL: b} for a, b in x_peers]
    friends += [{Z: (z + k) % NZ} for k in range(1, NZ)]
    for friend in friends:
        pl.semaphore_signal(barrier, inc=1, device_id=friend, device_id_type=pl.DeviceIdType.MESH)

    load_feat.wait()
    for k in range(DIN // LANES):
        part = feat[:, k * LANES:(k + 1) * LANES]
        ft[me, k * LANES:(k + 1) * LANES, :] = part.T

    pl.semaphore_wait(barrier, len(friends))

    quarter = DIN // 4

    def feature(direction, q, late):
        ref = ft.at[me, pl.ds(q * quarter, quarter)]
        send(ref, ref, f_s.at[direction], f_r.at[late, direction], {Y: yp if direction == 0 else ym})

    feature(0, 0, 0)
    feature(1, 2, 0)
    def side(o):
        return xh if o == 0 else oxh

    def weights_on(direction, block, step, o):
        ref = wf.at[block, side(o), c]
        send(ref, ref, wz_s.at[0], wz_r.at[direction, step - 1, o], {Z: zp if direction == 0 else zm})

    def weights_next(step, o, start=True):
        blocks = [(z + NZ - step) % NZ, (z + step) % NZ]
        for direction, b in enumerate(blocks):
            if start:
                arrived(wf.at[b, side(o), c], wz_r.at[direction, step - 1, o])
            if step < 3:
                weights_on(direction, b, step + 1, o)
        if step == 3:
            for direction, b in enumerate(blocks):
                ref = wf.at[b, side(o), c, pl.ds(direction * 16, 16)]
                send(ref, ref, wz_s.at[0], wl_r.at[o], {Z: zp if direction == 0 else zm})
        for b in blocks:
            ref = wf.at[b, side(o), c]
            send(ref, ref, wp_s.at[0], wp_r.at[step - 1], partner)

    def weights_over():
        outer = {XH: oxh, XL: oxl}
        for direction, b in enumerate(((z + NZ - 1) % NZ, (z + 1) % NZ)):
            ref = wf.at[b, xh, c]
            arrived(ref, wz_r.at[direction, 0, 0])
            send(ref, ref, wo_s.at[0], wz_r.at[direction, 0, 1], outer)
        send(wf.at[z, xh, c], wf.at[z, xh, c], wo_s.at[0], wo_r.at[0], outer)

    def weights_last(o):
        ref = wf.at[(z + 4) % NZ, side(o), c]
        arrived(ref, wl_r.at[o])
        send(ref, ref, wp_s.at[0], wp_r.at[3], partner)

    load_w.wait()
    weights_on(0, z, 1, 0)
    weights_on(1, z, 1, 0)

    per_group = BLOCKS // GROUPS
    for group in range(GROUPS):
        for copy in loads[group]:
            copy.wait()

        def sums(i, carry):
            b = group * per_group + i
            cols = pl.ds(pl.multiple_of(b * LANES, LANES), LANES)
            value = jnp.where(mask[:, cols] != 0, cot[:, cols].astype(F32), 0.0)
            msk[b] = value.astype(BF16)
            half, row = b // HALF, b % HALF
            st[half, pl.ds(row, 1), :] = jnp.sum(value, axis=0, keepdims=True)
            cross = value * normed[:, cols].astype(F32)
            st[half, pl.ds(HALF + row, 1), :] = jnp.sum(cross, axis=0, keepdims=True)
            return carry

        lax.fori_loop(0, per_group, sums, 0)

    send(st.at[oc], st_core.at[c], stat_s.at[0], stat_r.at[0], partner)
    arrived(st_core.at[oc], stat_r.at[0])
    st_y[y] = st[c] + st_core[oc]
    for k in (2, 1, 3):
        send(st_y.at[y], st_y.at[y], stat_s.at[1], stat_r.at[1], {Y: (y + k) % NY})
    feature(0, 1, 0)
    feature(1, 3, 0)
    for late in ((2, 1), (3, 0)):
        for direction in range(2):
            feature(direction, late[direction], 1)
    arrived(st_y.at[pl.ds(0, NY - 1)], stat_r.at[1])
    st_x[x] = st_y[0] + st_y[1] + st_y[2] + st_y[3]
    for a, b in x_peers:
        send(st_x.at[x], st_x.at[x], stat_s.at[2], stat_r.at[2], {XH: a, XL: b})
    weights_over()
    arrived(st_x.at[pl.ds(0, NX - 1)], stat_r.at[2])
    st_z[z] = st_x[0] + st_x[1] + st_x[2] + st_x[3]
    for k in (4, 3, 5, 2, 6, 1, 7):
        send(st_z.at[z], st_z.at[z], stat_s.at[3], stat_r.at[3], {Z: (z + k) % NZ})
    mid = DIN // 2
    low, high = ft.at[2 * ym + c, pl.ds(0, mid)], ft.at[2 * yp + c, pl.ds(mid, mid)]
    arrived(low, f_r.at[0, 0])
    send(low, low, f_s.at[2], f_r.at[2, 0], {Y: yp})
    arrived(high, f_r.at[0, 1])
    send(high, high, f_s.at[3], f_r.at[2, 1], {Y: ym})
    weights_next(1, 0, start=False)
    arrived(st_z.at[pl.ds(0, NZ - 1)], stat_r.at[3])
    st_all[c] = sum((st_z[k] for k in range(1, NZ)), st_z[0])
    send(st_all.at[c], st_all.at[c], stat_s.at[4], stat_r.at[4], partner)
    send(ft.at[me], ft.at[me], fp_s.at[0], fp_r.at[0], partner)
    load_a.wait()
    load_b.wait()
    arrived(st_all.at[oc], stat_r.at[4])
    store_stat = pltpu.make_async_copy(st_all, stat_hbm, out_sem.at[0])
    store_stat.start()

    inverse_rows = 1.0 / (ROWS * NZ * NX * NY * 2)

    def norm_grad(j):
        def one(i, carry):
            b = i * CHUNKS + j
            cols = pl.ds(pl.multiple_of(b * LANES, LANES), LANES)
            half, row = b // HALF, b % HALF
            plain = st_all[half, pl.ds(row, 1), :] * inverse_rows
            cross = st_all[half, pl.ds(HALF + row, 1), :] * inverse_rows
            scale = scale_b[pl.ds(b, 1), :] * scale_a[pl.ds(b, 1), :]
            value = msk[b].astype(F32) - plain - normed[:, cols].astype(F32) * cross
            ngs[b] = (scale * value).astype(BF16)
            return carry

        lax.fori_loop(0, NY * 2, one, 0)
        ngr[j, me] = ngs[me * CHUNKS + j]

    def block(chip, core, j):
        return ngs.at[(chip * 2 + core) * CHUNKS + j]

    def send_far(j):
        send(block(y2, 0, j), rel.at[0, j], ng_s.at[j], rel_r.at[0, j], {Y: yp})
        send(block(y2, 1, j), rel.at[1, j], ng_s.at[j], rel_r.at[1, j], {Y: ym})

    def send_near_to(j, chip, core):
        send(block(chip, core, j), ngr.at[j, me], ng_s.at[j], near_r.at[j], {Y: chip, C: core})

    def send_near(j, cores=(0, 1)):
        for core in cores:
            for chip in (yp, ym):
                send_near_to(j, chip, core)
        send(block(y, oc, j), ngr.at[j, me], ng_s.at[j], near_r.at[j], partner)

    def pass_on(j, late=False):
        arrived(rel.at[0, j], rel_r.at[0, j])
        send(rel.at[0, j], ngr.at[j, 2 * ym + c], ng_s.at[j], far_r.at[j], {Y: yp, C: 0})
        if late:
            send_near_to(j, yp, 1)
            send_near_to(j, ym, 1)
        arrived(rel.at[1, j], rel_r.at[1, j])
        send(rel.at[1, j], ngr.at[j, 2 * yp + c], ng_s.at[j], far_r.at[j], {Y: ym, C: 1})

    tall = 256

    def product(j, rows, sources):
        a = jnp.concatenate([ft[s, rows, :] for s in sources], axis=1)
        b = jnp.concatenate([ngr[j, s] for s in sources], axis=0)
        return jnp.dot(a, b, preferred_element_type=F32)

    def multiply_near(j):
        arrived(ngr.at[j, pl.ds(0, 5)], near_r.at[j])

        def tile(i, carry):
            rows = pl.ds(pl.multiple_of(i * tall, tall), tall)
            near[rows, :] = product(j, rows, [2 * chip + core for chip in (y, yp, ym) for core in range(2)])
            return carry

        lax.fori_loop(0, DIN // tall, tile, 0)

    def multiply_far(j):
        arrived(ngr.at[j, pl.ds(0, 2)], far_r.at[j])

        def tile(i, carry):
            rows = pl.ds(pl.multiple_of(i * tall, tall), tall)
            out = (near[rows, :] + product(j, rows, [2 * y2, 2 * y2 + 1])).astype(STAGE_X)
            each = DIN // NZ
            share = each // NX
            for a in range(tall // each):
                for b in range(NX):
                    xs[j, b, i * (tall // each) + a] = out[a * each + b * share:a * each + (b + 1) * share]
            ready = pl.ds(i * (tall // each), tall // each)
            for a, b in x_peers:
                send(xs.at[j, 2 * a + b, ready], xr.at[j, x, ready], x_s.at[j], x_r.at[j], {XH: a, XL: b})
            return carry

        lax.fori_loop(0, DIN // tall, tile, 0)
        xr[j, x] = xs[j, x]

    def over_x(j):
        arrived(xr.at[j, pl.ds(0, NX - 1)], x_r.at[j])
        total = xr[j, 0].astype(F32)
        for k in range(1, NX):
            total += xr[j, k].astype(F32)
        zs[j] = total.astype(STAGE_Z)
        for k in (4, 3, 5, 2, 6, 1, 7):
            to = (z + k) % NZ
            send(zs.at[j, to], zr.at[j, z], z_s.at[j], z_r.at[j], {Z: to})
        zr[j, z] = zs[j, z]

    others = [(chip, lane) for chip in (y2, yp, ym) for lane in (oxl, xl)] + [(y, oxl)]

    def over_z(j):
        arrived(zr.at[j, pl.ds(0, NZ - 1)], z_r.at[j])
        total = zr[j, 0].astype(F32)
        for k in range(1, NZ):
            total += zr[j, k].astype(F32)
        gw[xl, y, c, j] = total
        mine = gw.at[xl, y, c, j]
        for chip, lane in others:
            send(mine, mine, g_s.at[j], g_r.at[j], {Y: chip, XL: lane})

    def gathered(j):
        arrived(near.at[pl.ds(0, len(others) * 32)], g_r.at[j])
        part = gw.at[:, :, c, j]
        send(part, part, gp_s.at[0], gp_r.at[j], partner)

    def grad_input(step):
        if step == 4:
            arrived(wf.at[pl.ds(0, 3), 0, 0], wp_r.at[3])
            blocks = (z, (z + 4) % NZ)
        else:
            arrived(wf.at[pl.ds(0, 2), :, 0], wp_r.at[step - 1])
            blocks = ((z - step + NZ) % NZ, (z + step) % NZ)
        acc[...] = jnp.zeros_like(acc)
        deep = 1024

        def part(i, carry):
            cols = pl.ds(pl.multiple_of(i * deep, deep), deep)
            count = deep // LANES
            a = jnp.concatenate([ngs[i * count + k] for k in range(count)], axis=1)
            b = jnp.concatenate([wf[k, :, :, :, cols].reshape(LANES, deep) for k in blocks], axis=0)
            acc[...] += lax.dot_general(a, b, (((1,), (1,)), ((), ())), preferred_element_type=F32)
            return carry

        lax.fori_loop(0, DOUT // deep, part, 0)
        for k, place in enumerate(blocks):
            cols = pl.ds(pl.multiple_of(place * LANES, LANES), LANES)
            gi[:, cols] = acc[:, k * LANES:(k + 1) * LANES].astype(BF16)

    def store(j):
        arrived(gw.at[:, :, oc, j], gp_r.at[j])
        copy = pltpu.make_async_copy(gw.at[:, :, :, j], gw_hbm.at[:, :, :, j], out_sem.at[2 + j])
        copy.start()
        return copy

    norm_grad(0)
    send_far(0)
    send_near(0)
    norm_grad(1)
    send_far(1)
    norm_grad(2)
    norm_grad(3)
    arrived(ft.at[2 * ym + c, pl.ds(0, mid)], f_r.at[1, 0])
    arrived(ft.at[2 * yp + c, pl.ds(0, mid)], f_r.at[1, 1])
    for chip in (ym, yp):
        send(ft.at[2 * chip + c], ft.at[2 * chip + c], fp_s.at[0], fp_r.at[0], partner)
    pass_on(0)
    send_far(2)
    send_near(1)
    weights_next(1, 1)
    weights_next(2, 0)
    for direction in range(2):
        arrived(ft.at[2 * y2 + c, pl.ds(direction * mid, mid)], f_r.at[2, direction])
    send(ft.at[2 * y2 + c], ft.at[2 * y2 + c], fp_s.at[0], fp_r.at[0], partner)
    pass_on(1)
    send_far(3)
    send_near(2)
    far_out = wf.at[z, oxh, c]
    arrived(far_out, wo_r.at[0])
    send(far_out, far_out, wp_s.at[1], wp_r.at[3], partner)
    arrived(ft.at[pl.ds(0, 4)], fp_r.at[0])
    multiply_near(0)
    multiply_far(0)
    send_near(3, (0,))
    pass_on(2)
    multiply_near(1)
    weights_next(2, 1)
    multiply_far(1)
    pass_on(3, late=True)
    over_x(0)
    grad_input(1)
    weights_next(3, 0)
    multiply_near(2)
    multiply_far(2)
    over_x(1)
    weights_next(3, 1)
    multiply_near(3)
    multiply_far(3)
    over_z(0)
    over_x(2)
    grad_input(2)
    weights_last(0)
    over_z(1)
    over_x(3)
    grad_input(3)
    over_z(2)
    weights_last(1)
    gathered(0)
    over_z(3)
    grad_input(4)
    store_gi = pltpu.make_async_copy(gi, gi_hbm, out_sem.at[1])
    store_gi.start()
    gathered(1)
    gathered(2)
    stores = [store(j) for j in range(CHUNKS - 2)]
    gathered(3)
    stores += [store(j) for j in range(CHUNKS - 2, CHUNKS)]

    left(st.at[0], stat_s.at[0])
    left(st_y.at[pl.ds(0, NY - 1)], stat_s.at[1])
    left(st_x.at[pl.ds(0, NX - 1)], stat_s.at[2])
    left(st_z.at[pl.ds(0, NZ - 1)], stat_s.at[3])
    left(st.at[0], stat_s.at[4])
    for direction in range(2):
        left(ft.at[0], f_s.at[direction])
        left(low, f_s.at[2 + direction])
    left(ft.at[pl.ds(0, 4)], fp_s.at[0])
    left(wf.at[pl.ds(0, 3), 0, 0], wo_s.at[0])
    left(wf.at[pl.ds(0, 6), :, 0], wz_s.at[0])
    left(wf.at[pl.ds(0, 7), :, 0], wp_s.at[0])
    left(far_out, wp_s.at[1])
    for j in range(CHUNKS):
        left(ngs.at[pl.ds(0, 9)], ng_s.at[j])
        left(xr.at[j, pl.ds(0, NX - 1)], x_s.at[j])
        left(zr.at[j, pl.ds(0, NZ - 1)], z_s.at[j])
        left(near.at[pl.ds(0, len(others) * 32)], g_s.at[j])
    left(gw.at[:, :, c], gp_s.at[0])
    store_stat.wait()
    store_gi.wait()
    for copy in stores:
        copy.wait()


def finish(rescale, gi, gw, stat, gi_out, gw_out, gain_out, shift_out, gi_v, gw_v, stat_v, full, gain, shift, sems):
    parts = gw_v.shape[0]
    count = BLOCKS // (parts // 2)
    tall = gw.shape[2]

    def source(k):
        return gw.at[k // 2, pl.ds(k % 2 * count, count)]

    def target(k):
        return gw_out.at[pl.ds(k // 2 * tall, tall), pl.ds(k % 2 * count * LANES, count * LANES)]

    loads = [pltpu.make_async_copy(source(k), gw_v.at[k], sems.at[k]) for k in range(parts)]
    loads.append(pltpu.make_async_copy(gi, gi_v, sems.at[parts]))
    loads.append(pltpu.make_async_copy(stat, stat_v, sems.at[parts + 1]))
    for copy in loads:
        copy.start()
    stores = []

    def put(src, dst, sem):
        stores.append(pltpu.make_async_copy(src, dst, sem))
        stores[-1].start()

    for k in range(parts):
        loads[k].wait()
        for b in range(count):
            full[k, :, b * LANES:(b + 1) * LANES] = gw_v[k, b] * rescale
        put(full.at[k], target(k), sems.at[parts + 2 + k])
    loads[parts].wait()
    put(gi_v, gi_out, sems.at[2 * parts + 2])
    loads[parts + 1].wait()
    for half in range(2):
        rows = slice(half * HALF, (half + 1) * HALF)
        shift[rows, :] = stat_v[half, :HALF] * rescale
        gain[rows, :] = stat_v[half, HALF:] * rescale
    put(gain, gain_out, sems.at[2 * parts + 3])
    put(shift, shift_out, sems.at[2 * parts + 4])
    for copy in stores:
        copy.wait()


def on_device(features, normed, relu_mask, cotangent, weight_shard, norm_gain, inverse_deviation):
    dma = pltpu.SemaphoreType.DMA
    vmem = pltpu.VMEM
    any_space = pl.BlockSpec(memory_space=pl.ANY)
    rows_out = DIN // (NZ * NX)
    scratch = [
        vmem((ROWS, DIN), BF16), vmem((ROWS, DOUT), BF16), vmem((ROWS, DOUT), jnp.int32), vmem((ROWS, DOUT), BF16),
        vmem((BLOCKS, LANES), F32), vmem((BLOCKS, LANES), F32), vmem((BLOCKS, ROWS, LANES), BF16),
        vmem((NZ, 2, 2, 32, DOUT), BF16), vmem((NY * 2, DIN, ROWS), BF16),
        vmem((BLOCKS, ROWS, LANES), BF16), vmem((CHUNKS, NY * 2, ROWS, LANES), BF16), vmem((2, CHUNKS, ROWS, LANES), BF16),
        vmem((CHUNKS, NX, NZ, rows_out, LANES), STAGE_X), vmem((CHUNKS, NX, NZ, rows_out, LANES), STAGE_X),
        vmem((CHUNKS, NZ, rows_out, LANES), STAGE_Z), vmem((CHUNKS, NZ, rows_out, LANES), STAGE_Z),
        vmem((2, NY, 2, CHUNKS, rows_out, LANES), F32), vmem((ROWS, DIN), BF16), vmem((ROWS, 256), F32),
        vmem((DIN, LANES), F32),
        vmem((2, BLOCKS, LANES), F32), vmem((2, BLOCKS, LANES), F32), vmem((NX, BLOCKS, LANES), F32),
        vmem((NY, BLOCKS, LANES), F32), vmem((NZ, BLOCKS, LANES), F32), vmem((2, BLOCKS, LANES), F32),
        dma((4 + 3 * GROUPS,)), dma((2 + CHUNKS,)), dma((5,)), dma((5,)),
        dma((4,)), dma((3, 2)), dma((1,)), dma((1,)),
        dma((1,)), dma((1,)), dma((1,)), dma((2, 3, 2)), dma((2,)), dma((2,)), dma((4,)),
        dma((CHUNKS,)), dma((CHUNKS,)), dma((CHUNKS,)), dma((2, CHUNKS)),
        dma((CHUNKS,)), dma((CHUNKS,)), dma((CHUNKS,)), dma((CHUNKS,)), dma((CHUNKS,)), dma((CHUNKS,)), dma((1,)), dma((CHUNKS,)),
    ]
    grad_input, pieces, sums = pl.pallas_call(
        body,
        out_shape=(
            jax.ShapeDtypeStruct((ROWS, DIN), BF16),
            jax.ShapeDtypeStruct((2, NY, 2, CHUNKS, rows_out, LANES), F32),
            jax.ShapeDtypeStruct((2, BLOCKS, LANES), F32),
        ),
        in_specs=[any_space] * 7,
        out_specs=(any_space,) * 3,
        scratch_shapes=scratch,
        compiler_params=pltpu.CompilerParams(
            collective_id=0, has_side_effects=True, vmem_limit_bytes=56 * 1024 * 1024,
        ),
    )(
        features, normed, relu_mask, cotangent, weight_shard.reshape(2, 32, DOUT),
        norm_gain.reshape(BLOCKS, LANES), inverse_deviation.reshape(BLOCKS, LANES),
    )
    steps = 4
    rescale = 1.0 / math.sqrt(ROWS * NZ * NX * NY * 2)
    grad_input, grad_weight, grad_gain, grad_shift = pl.pallas_call(
        functools.partial(finish, rescale),
        out_shape=(
            jax.ShapeDtypeStruct((ROWS, DIN), BF16),
            jax.ShapeDtypeStruct((2 * rows_out, DOUT), F32),
            jax.ShapeDtypeStruct((BLOCKS, LANES), F32),
            jax.ShapeDtypeStruct((BLOCKS, LANES), F32),
        ),
        in_specs=[any_space] * 3,
        out_specs=(any_space,) * 4,
        scratch_shapes=[
            vmem((ROWS, DIN), BF16), vmem((steps, 2 * BLOCKS // steps, rows_out, LANES), F32), vmem((2, BLOCKS, LANES), F32),
            vmem((steps, rows_out, DOUT * 2 // steps), F32), vmem((BLOCKS, LANES), F32), vmem((BLOCKS, LANES), F32),
            dma((2 * steps + 5,)),
        ],
    )(grad_input, pieces.reshape(2, BLOCKS, rows_out, LANES), sums)
    return grad_input, grad_weight, grad_gain.reshape(DOUT), grad_shift.reshape(DOUT)


def solution(mesh):
    split = Mesh(mesh.devices.reshape(NZ, 2, NY, 2, 2), (Z, XH, Y, XL, C))
    rows = P((Z, XH, Y, XL, C), None)
    shard = P((Z, XH), None)
    return jax.shard_map(
        on_device,
        mesh=split,
        in_specs=(rows, rows, rows, rows, shard, P(), P()),
        out_specs=(rows, shard, P(), P()),
        check_vma=False,
    )
```

```python
import functools
import math

import jax
import jax.numpy as jnp
from jax import lax
from jax.experimental import pallas as pl
from jax.experimental.pallas import tpu as pltpu
from jax.sharding import Mesh
from jax.sharding import PartitionSpec as P

Z, XH, Y, XL, C = "z", "xh", "y", "xl", "c"
NZ, NX, NY = 8, 4, 4
F32, BF16 = jnp.float32, jnp.bfloat16

ROWS = 256
DIN = 1024
DOUT = 4096
LANES = 128
BLOCKS = DOUT // LANES
CHUNKS = BLOCKS // (NY * 2)
HALF = BLOCKS // 2
GROUPS = 4

STAGE_X = BF16
STAGE_Z = BF16


def body(
    feat_hbm, normed_hbm, mask_hbm, cot_hbm, w_hbm, gain_hbm, inv_hbm,
    gi_hbm, gw_hbm, stat_hbm,
    feat, normed, mask, cot, scale_a, scale_b, msk, wf, ft, ngs, ngr, rel,
    xs, xr, zs, zr, gw, gi, acc, near, st, st_core, st_x, st_y, st_z, st_all,
    load_sem, out_sem, stat_s, stat_r,
    f_s, f_r, fp_s, fp_r,
    wo_s, wo_r, wz_s, wz_r, wl_r, wp_s, wp_r,
    ng_s, near_r, far_r, rel_r,
    x_s, x_r, z_s, z_r, g_s, g_r, gp_s, gp_r,
):
    z, xh, y, xl, c = (lax.axis_index(name) for name in (Z, XH, Y, XL, C))
    x = 2 * xh + xl
    oc, oxh, oxl = 1 - c, 1 - xh, 1 - xl
    yp, ym, y2 = (y + 1) % NY, (y + 3) % NY, (y + 2) % NY
    zp, zm = (z + 1) % NZ, (z + NZ - 1) % NZ
    me = 2 * y + c
    partner = {C: oc}
    x_peers = [(oxh, xl), (oxh, oxl), (xh, oxl)]

    def remote(src, dst, ss, rs, device):
        return pltpu.make_async_remote_copy(
            src_ref=src, dst_ref=dst, send_sem=ss, recv_sem=rs,
            device_id=device, device_id_type=pl.DeviceIdType.MESH,
        )

    def send(src, dst, ss, rs, device):
        remote(src, dst, ss, rs, device).start()

    def arrived(ref, rs):
        remote(ref, ref, rs, rs, partner).wait_recv()

    def left(ref, ss):
        remote(ref, ref, ss, ss, partner).wait_send()

    load_feat = pltpu.make_async_copy(feat_hbm, feat, load_sem.at[0])
    load_w = pltpu.make_async_copy(w_hbm, wf.at[z, xh], load_sem.at[1])
    load_a = pltpu.make_async_copy(gain_hbm, scale_a, load_sem.at[2])
    load_b = pltpu.make_async_copy(inv_hbm, scale_b, load_sem.at[3])
    loads = []
    width = DOUT // GROUPS
    load_feat.start()
    load_w.start()
    for group in range(GROUPS):
        cols = pl.ds(group * width, width)
        loads.append([
            pltpu.make_async_copy(src.at[:, cols], dst.at[:, cols], load_sem.at[4 + 3 * group + k])
            for k, (src, dst) in enumerate(((cot_hbm, cot), (mask_hbm, mask), (normed_hbm, normed)))
        ])
        for copy in loads[-1]:
            copy.start()
    load_a.start()
    load_b.start()

    barrier = pltpu.get_barrier_semaphore()
    friends = [partner]
    for other in (yp, ym, y2):
        friends += [{Y: other, C: c}, {Y: other, C: oc}, {Y: other, XL: oxl}]
    friends += [{XH: a, XL: b} for a, b in x_peers]
    friends += [{Z: (z + k) % NZ} for k in range(1, NZ)]
    for friend in friends:
        pl.semaphore_signal(barrier, inc=1, device_id=friend, device_id_type=pl.DeviceIdType.MESH)

    load_feat.wait()
    for k in range(DIN // LANES):
        part = feat[:, k * LANES:(k + 1) * LANES]
        ft[me, k * LANES:(k + 1) * LANES, :] = part.T

    pl.semaphore_wait(barrier, len(friends))

    quarter = DIN // 4

    def feature(direction, q, late):
        ref = ft.at[me, pl.ds(q * quarter, quarter)]
        send(ref, ref, f_s.at[direction], f_r.at[late, direction], {Y: yp if direction == 0 else ym})

    feature(0, 0, 0)
    feature(1, 2, 0)
    def side(o):
        return xh if o == 0 else oxh

    def weights_on(direction, block, step, o):
        ref = wf.at[block, side(o), c]
        send(ref, ref, wz_s.at[0], wz_r.at[direction, step - 1, o], {Z: zp if direction == 0 else zm})

    def weights_next(step, o, start=True):
        blocks = [(z + NZ - step) % NZ, (z + step) % NZ]
        for direction, b in enumerate(blocks):
            if start:
                arrived(wf.at[b, side(o), c], wz_r.at[direction, step - 1, o])
            if step < 3:
                weights_on(direction, b, step + 1, o)
        if step == 3:
            for direction, b in enumerate(blocks):
                ref = wf.at[b, side(o), c, pl.ds(direction * 16, 16)]
                send(ref, ref, wz_s.at[0], wl_r.at[o], {Z: zp if direction == 0 else zm})
        for b in blocks:
            ref = wf.at[b, side(o), c]
            send(ref, ref, wp_s.at[0], wp_r.at[step - 1], partner)

    def weights_over():
        outer = {XH: oxh, XL: oxl}
        for direction, b in enumerate(((z + NZ - 1) % NZ, (z + 1) % NZ)):
            ref = wf.at[b, xh, c]
            arrived(ref, wz_r.at[direction, 0, 0])
            send(ref, ref, wo_s.at[0], wz_r.at[direction, 0, 1], outer)
        send(wf.at[z, xh, c], wf.at[z, xh, c], wo_s.at[0], wo_r.at[0], outer)

    def weights_last(o):
        ref = wf.at[(z + 4) % NZ, side(o), c]
        arrived(ref, wl_r.at[o])
        send(ref, ref, wp_s.at[0], wp_r.at[3], partner)

    load_w.wait()
    weights_on(0, z, 1, 0)
    weights_on(1, z, 1, 0)

    per_group = BLOCKS // GROUPS
    for group in range(GROUPS):
        for copy in loads[group]:
            copy.wait()

        def sums(i, carry):
            b = group * per_group + i
            cols = pl.ds(pl.multiple_of(b * LANES, LANES), LANES)
            value = jnp.where(mask[:, cols] != 0, cot[:, cols].astype(F32), 0.0)
            msk[b] = value.astype(BF16)
            half, row = b // HALF, b % HALF
            st[half, pl.ds(row, 1), :] = jnp.sum(value, axis=0, keepdims=True)
            cross = value * normed[:, cols].astype(F32)
            st[half, pl.ds(HALF + row, 1), :] = jnp.sum(cross, axis=0, keepdims=True)
            return carry

        lax.fori_loop(0, per_group, sums, 0)

    send(st.at[oc], st_core.at[c], stat_s.at[0], stat_r.at[0], partner)
    arrived(st_core.at[oc], stat_r.at[0])
    st_y[y] = st[c] + st_core[oc]
    for k in (2, 1, 3):
        send(st_y.at[y], st_y.at[y], stat_s.at[1], stat_r.at[1], {Y: (y + k) % NY})
    feature(0, 1, 0)
    feature(1, 3, 0)
    for late in ((2, 1), (3, 0)):
        for direction in range(2):
            feature(direction, late[direction], 1)
    arrived(st_y.at[pl.ds(0, NY - 1)], stat_r.at[1])
    st_x[x] = st_y[0] + st_y[1] + st_y[2] + st_y[3]
    for a, b in x_peers:
        send(st_x.at[x], st_x.at[x], stat_s.at[2], stat_r.at[2], {XH: a, XL: b})
    weights_over()
    arrived(st_x.at[pl.ds(0, NX - 1)], stat_r.at[2])
    st_z[z] = st_x[0] + st_x[1] + st_x[2] + st_x[3]
    for k in (4, 3, 5, 2, 6, 1, 7):
        send(st_z.at[z], st_z.at[z], stat_s.at[3], stat_r.at[3], {Z: (z + k) % NZ})
    mid = DIN // 2
    low, high = ft.at[2 * ym + c, pl.ds(0, mid)], ft.at[2 * yp + c, pl.ds(mid, mid)]
    arrived(low, f_r.at[0, 0])
    send(low, low, f_s.at[2], f_r.at[2, 0], {Y: yp})
    arrived(high, f_r.at[0, 1])
    send(high, high, f_s.at[3], f_r.at[2, 1], {Y: ym})
    weights_next(1, 0, start=False)
    arrived(st_z.at[pl.ds(0, NZ - 1)], stat_r.at[3])
    st_all[c] = sum((st_z[k] for k in range(1, NZ)), st_z[0])
    send(st_all.at[c], st_all.at[c], stat_s.at[4], stat_r.at[4], partner)
    send(ft.at[me], ft.at[me], fp_s.at[0], fp_r.at[0], partner)
    load_a.wait()
    load_b.wait()
    arrived(st_all.at[oc], stat_r.at[4])
    store_stat = pltpu.make_async_copy(st_all, stat_hbm, out_sem.at[0])
    store_stat.start()

    inverse_rows = 1.0 / (ROWS * NZ * NX * NY * 2)

    def norm_grad(j):
        def one(i, carry):
            b = i * CHUNKS + j
            cols = pl.ds(pl.multiple_of(b * LANES, LANES), LANES)
            half, row = b // HALF, b % HALF
            plain = st_all[half, pl.ds(row, 1), :] * inverse_rows
            cross = st_all[half, pl.ds(HALF + row, 1), :] * inverse_rows
            scale = scale_b[pl.ds(b, 1), :] * scale_a[pl.ds(b, 1), :]
            value = msk[b].astype(F32) - plain - normed[:, cols].astype(F32) * cross
            ngs[b] = (scale * value).astype(BF16)
            return carry

        lax.fori_loop(0, NY * 2, one, 0)
        ngr[j, me] = ngs[me * CHUNKS + j]

    def block(chip, core, j):
        return ngs.at[(chip * 2 + core) * CHUNKS + j]

    def send_far(j):
        send(block(y2, 0, j), rel.at[0, j], ng_s.at[j], rel_r.at[0, j], {Y: yp})
        send(block(y2, 1, j), rel.at[1, j], ng_s.at[j], rel_r.at[1, j], {Y: ym})

    def send_near_to(j, chip, core):
        send(block(chip, core, j), ngr.at[j, me], ng_s.at[j], near_r.at[j], {Y: chip, C: core})

    def send_near(j, cores=(0, 1)):
        for core in cores:
            for chip in (yp, ym):
                send_near_to(j, chip, core)
        send(block(y, oc, j), ngr.at[j, me], ng_s.at[j], near_r.at[j], partner)

    def pass_on(j, late=False):
        arrived(rel.at[0, j], rel_r.at[0, j])
        send(rel.at[0, j], ngr.at[j, 2 * ym + c], ng_s.at[j], far_r.at[j], {Y: yp, C: 0})
        if late:
            send_near_to(j, yp, 1)
            send_near_to(j, ym, 1)
        arrived(rel.at[1, j], rel_r.at[1, j])
        send(rel.at[1, j], ngr.at[j, 2 * yp + c], ng_s.at[j], far_r.at[j], {Y: ym, C: 1})

    tall = 256

    def product(j, rows, sources):
        a = jnp.concatenate([ft[s, rows, :] for s in sources], axis=1)
        b = jnp.concatenate([ngr[j, s] for s in sources], axis=0)
        return jnp.dot(a, b, preferred_element_type=F32)

    def multiply_near(j):
        arrived(ngr.at[j, pl.ds(0, 5)], near_r.at[j])

        def tile(i, carry):
            rows = pl.ds(pl.multiple_of(i * tall, tall), tall)
            near[rows, :] = product(j, rows, [2 * chip + core for chip in (y, yp, ym) for core in range(2)])
            return carry

        lax.fori_loop(0, DIN // tall, tile, 0)

    def multiply_far(j):
        arrived(ngr.at[j, pl.ds(0, 2)], far_r.at[j])

        def tile(i, carry):
            rows = pl.ds(pl.multiple_of(i * tall, tall), tall)
            out = (near[rows, :] + product(j, rows, [2 * y2, 2 * y2 + 1])).astype(STAGE_X)
            each = DIN // NZ
            share = each // NX
            for a in range(tall // each):
                for b in range(NX):
                    xs[j, b, i * (tall // each) + a] = out[a * each + b * share:a * each + (b + 1) * share]
            ready = pl.ds(i * (tall // each), tall // each)
            for a, b in x_peers:
                send(xs.at[j, 2 * a + b, ready], xr.at[j, x, ready], x_s.at[j], x_r.at[j], {XH: a, XL: b})
            return carry

        lax.fori_loop(0, DIN // tall, tile, 0)
        xr[j, x] = xs[j, x]

    def over_x(j):
        arrived(xr.at[j, pl.ds(0, NX - 1)], x_r.at[j])
        total = xr[j, 0].astype(F32)
        for k in range(1, NX):
            total += xr[j, k].astype(F32)
        zs[j] = total.astype(STAGE_Z)
        for k in (4, 3, 5, 2, 6, 1, 7):
            to = (z + k) % NZ
            send(zs.at[j, to], zr.at[j, z], z_s.at[j], z_r.at[j], {Z: to})
        zr[j, z] = zs[j, z]

    others = [(chip, lane) for chip in (y2, yp, ym) for lane in (oxl, xl)] + [(y, oxl)]

    def over_z(j):
        arrived(zr.at[j, pl.ds(0, NZ - 1)], z_r.at[j])
        total = zr[j, 0].astype(F32)
        for k in range(1, NZ):
            total += zr[j, k].astype(F32)
        gw[xl, y, c, j] = total
        mine = gw.at[xl, y, c, j]
        for chip, lane in others:
            send(mine, mine, g_s.at[j], g_r.at[j], {Y: chip, XL: lane})

    def gathered(j):
        arrived(near.at[pl.ds(0, len(others) * 32)], g_r.at[j])
        part = gw.at[:, :, c, j]
        send(part, part, gp_s.at[0], gp_r.at[j], partner)

    def grad_input(step):
        if step == 4:
            arrived(wf.at[pl.ds(0, 3), 0, 0], wp_r.at[3])
            blocks = (z, (z + 4) % NZ)
        else:
            arrived(wf.at[pl.ds(0, 2), :, 0], wp_r.at[step - 1])
            blocks = ((z - step + NZ) % NZ, (z + step) % NZ)
        acc[...] = jnp.zeros_like(acc)
        deep = 1024

        def part(i, carry):
            cols = pl.ds(pl.multiple_of(i * deep, deep), deep)
            count = deep // LANES
            a = jnp.concatenate([ngs[i * count + k] for k in range(count)], axis=1)
            b = jnp.concatenate([wf[k, :, :, :, cols].reshape(LANES, deep) for k in blocks], axis=0)
            acc[...] += lax.dot_general(a, b, (((1,), (1,)), ((), ())), preferred_element_type=F32)
            return carry

        lax.fori_loop(0, DOUT // deep, part, 0)
        for k, place in enumerate(blocks):
            cols = pl.ds(pl.multiple_of(place * LANES, LANES), LANES)
            gi[:, cols] = acc[:, k * LANES:(k + 1) * LANES].astype(BF16)

    def store(j):
        arrived(gw.at[:, :, oc, j], gp_r.at[j])
        copy = pltpu.make_async_copy(gw.at[:, :, :, j], gw_hbm.at[:, :, :, j], out_sem.at[2 + j])
        copy.start()
        return copy

    norm_grad(0)
    send_far(0)
    send_near(0)
    norm_grad(1)
    send_far(1)
    norm_grad(2)
    norm_grad(3)
    arrived(ft.at[2 * ym + c, pl.ds(0, mid)], f_r.at[1, 0])
    arrived(ft.at[2 * yp + c, pl.ds(0, mid)], f_r.at[1, 1])
    for chip in (ym, yp):
        send(ft.at[2 * chip + c], ft.at[2 * chip + c], fp_s.at[0], fp_r.at[0], partner)
    pass_on(0)
    send_far(2)
    send_near(1)
    weights_next(1, 1)
    weights_next(2, 0)
    for direction in range(2):
        arrived(ft.at[2 * y2 + c, pl.ds(direction * mid, mid)], f_r.at[2, direction])
    send(ft.at[2 * y2 + c], ft.at[2 * y2 + c], fp_s.at[0], fp_r.at[0], partner)
    pass_on(1)
    send_far(3)
    send_near(2)
    far_out = wf.at[z, oxh, c]
    arrived(far_out, wo_r.at[0])
    send(far_out, far_out, wp_s.at[1], wp_r.at[3], partner)
    arrived(ft.at[pl.ds(0, 4)], fp_r.at[0])
    multiply_near(0)
    multiply_far(0)
    send_near(3, (0,))
    pass_on(2)
    multiply_near(1)
    weights_next(2, 1)
    multiply_far(1)
    pass_on(3, late=True)
    over_x(0)
    grad_input(1)
    weights_next(3, 0)
    multiply_near(2)
    multiply_far(2)
    over_x(1)
    multiply_near(3)
    multiply_far(3)
    weights_next(3, 1)
    over_z(0)
    over_x(2)
    grad_input(2)
    weights_last(0)
    over_z(1)
    over_x(3)
    grad_input(3)
    over_z(2)
    weights_last(1)
    gathered(0)
    over_z(3)
    grad_input(4)
    store_gi = pltpu.make_async_copy(gi, gi_hbm, out_sem.at[1])
    store_gi.start()
    gathered(1)
    gathered(2)
    stores = [store(j) for j in range(CHUNKS - 2)]
    gathered(3)
    stores += [store(j) for j in range(CHUNKS - 2, CHUNKS)]

    left(st.at[0], stat_s.at[0])
    left(st_y.at[pl.ds(0, NY - 1)], stat_s.at[1])
    left(st_x.at[pl.ds(0, NX - 1)], stat_s.at[2])
    left(st_z.at[pl.ds(0, NZ - 1)], stat_s.at[3])
    left(st.at[0], stat_s.at[4])
    for direction in range(2):
        left(ft.at[0], f_s.at[direction])
        left(low, f_s.at[2 + direction])
    left(ft.at[pl.ds(0, 4)], fp_s.at[0])
    left(wf.at[pl.ds(0, 3), 0, 0], wo_s.at[0])
    left(wf.at[pl.ds(0, 6), :, 0], wz_s.at[0])
    left(wf.at[pl.ds(0, 7), :, 0], wp_s.at[0])
    left(far_out, wp_s.at[1])
    for j in range(CHUNKS):
        left(ngs.at[pl.ds(0, 9)], ng_s.at[j])
        left(xr.at[j, pl.ds(0, NX - 1)], x_s.at[j])
        left(zr.at[j, pl.ds(0, NZ - 1)], z_s.at[j])
        left(near.at[pl.ds(0, len(others) * 32)], g_s.at[j])
    left(gw.at[:, :, c], gp_s.at[0])
    store_stat.wait()
    store_gi.wait()
    for copy in stores:
        copy.wait()


def finish(rescale, gi, gw, stat, gi_out, gw_out, gain_out, shift_out, gi_v, gw_v, stat_v, full, gain, shift, sems):
    parts = gw_v.shape[0]
    count = BLOCKS // (parts // 2)
    tall = gw.shape[2]

    def source(k):
        return gw.at[k // 2, pl.ds(k % 2 * count, count)]

    def target(k):
        return gw_out.at[pl.ds(k // 2 * tall, tall), pl.ds(k % 2 * count * LANES, count * LANES)]

    loads = [pltpu.make_async_copy(source(k), gw_v.at[k], sems.at[k]) for k in range(parts)]
    loads.append(pltpu.make_async_copy(gi, gi_v, sems.at[parts]))
    loads.append(pltpu.make_async_copy(stat, stat_v, sems.at[parts + 1]))
    for copy in loads:
        copy.start()
    stores = []

    def put(src, dst, sem):
        stores.append(pltpu.make_async_copy(src, dst, sem))
        stores[-1].start()

    for k in range(parts):
        loads[k].wait()
        for b in range(count):
            full[k, :, b * LANES:(b + 1) * LANES] = gw_v[k, b] * rescale
        put(full.at[k], target(k), sems.at[parts + 2 + k])
    loads[parts].wait()
    put(gi_v, gi_out, sems.at[2 * parts + 2])
    loads[parts + 1].wait()
    for half in range(2):
        rows = slice(half * HALF, (half + 1) * HALF)
        shift[rows, :] = stat_v[half, :HALF] * rescale
        gain[rows, :] = stat_v[half, HALF:] * rescale
    put(gain, gain_out, sems.at[2 * parts + 3])
    put(shift, shift_out, sems.at[2 * parts + 4])
    for copy in stores:
        copy.wait()


def on_device(features, normed, relu_mask, cotangent, weight_shard, norm_gain, inverse_deviation):
    dma = pltpu.SemaphoreType.DMA
    vmem = pltpu.VMEM
    any_space = pl.BlockSpec(memory_space=pl.ANY)
    rows_out = DIN // (NZ * NX)
    scratch = [
        vmem((ROWS, DIN), BF16), vmem((ROWS, DOUT), BF16), vmem((ROWS, DOUT), jnp.int32), vmem((ROWS, DOUT), BF16),
        vmem((BLOCKS, LANES), F32), vmem((BLOCKS, LANES), F32), vmem((BLOCKS, ROWS, LANES), BF16),
        vmem((NZ, 2, 2, 32, DOUT), BF16), vmem((NY * 2, DIN, ROWS), BF16),
        vmem((BLOCKS, ROWS, LANES), BF16), vmem((CHUNKS, NY * 2, ROWS, LANES), BF16), vmem((2, CHUNKS, ROWS, LANES), BF16),
        vmem((CHUNKS, NX, NZ, rows_out, LANES), STAGE_X), vmem((CHUNKS, NX, NZ, rows_out, LANES), STAGE_X),
        vmem((CHUNKS, NZ, rows_out, LANES), STAGE_Z), vmem((CHUNKS, NZ, rows_out, LANES), STAGE_Z),
        vmem((2, NY, 2, CHUNKS, rows_out, LANES), F32), vmem((ROWS, DIN), BF16), vmem((ROWS, 256), F32),
        vmem((DIN, LANES), F32),
        vmem((2, BLOCKS, LANES), F32), vmem((2, BLOCKS, LANES), F32), vmem((NX, BLOCKS, LANES), F32),
        vmem((NY, BLOCKS, LANES), F32), vmem((NZ, BLOCKS, LANES), F32), vmem((2, BLOCKS, LANES), F32),
        dma((4 + 3 * GROUPS,)), dma((2 + CHUNKS,)), dma((5,)), dma((5,)),
        dma((4,)), dma((3, 2)), dma((1,)), dma((1,)),
        dma((1,)), dma((1,)), dma((1,)), dma((2, 3, 2)), dma((2,)), dma((2,)), dma((4,)),
        dma((CHUNKS,)), dma((CHUNKS,)), dma((CHUNKS,)), dma((2, CHUNKS)),
        dma((CHUNKS,)), dma((CHUNKS,)), dma((CHUNKS,)), dma((CHUNKS,)), dma((CHUNKS,)), dma((CHUNKS,)), dma((1,)), dma((CHUNKS,)),
    ]
    grad_input, pieces, sums = pl.pallas_call(
        body,
        out_shape=(
            jax.ShapeDtypeStruct((ROWS, DIN), BF16),
            jax.ShapeDtypeStruct((2, NY, 2, CHUNKS, rows_out, LANES), F32),
            jax.ShapeDtypeStruct((2, BLOCKS, LANES), F32),
        ),
        in_specs=[any_space] * 7,
        out_specs=(any_space,) * 3,
        scratch_shapes=scratch,
        compiler_params=pltpu.CompilerParams(
            collective_id=0, has_side_effects=True, vmem_limit_bytes=56 * 1024 * 1024,
        ),
    )(
        features, normed, relu_mask, cotangent, weight_shard.reshape(2, 32, DOUT),
        norm_gain.reshape(BLOCKS, LANES), inverse_deviation.reshape(BLOCKS, LANES),
    )
    steps = 4
    rescale = 1.0 / math.sqrt(ROWS * NZ * NX * NY * 2)
    grad_input, grad_weight, grad_gain, grad_shift = pl.pallas_call(
        functools.partial(finish, rescale),
        out_shape=(
            jax.ShapeDtypeStruct((ROWS, DIN), BF16),
            jax.ShapeDtypeStruct((2 * rows_out, DOUT), F32),
            jax.ShapeDtypeStruct((BLOCKS, LANES), F32),
            jax.ShapeDtypeStruct((BLOCKS, LANES), F32),
        ),
        in_specs=[any_space] * 3,
        out_specs=(any_space,) * 4,
        scratch_shapes=[
            vmem((ROWS, DIN), BF16), vmem((steps, 2 * BLOCKS // steps, rows_out, LANES), F32), vmem((2, BLOCKS, LANES), F32),
            vmem((steps, rows_out, DOUT * 2 // steps), F32), vmem((BLOCKS, LANES), F32), vmem((BLOCKS, LANES), F32),
            dma((2 * steps + 5,)),
        ],
    )(grad_input, pieces.reshape(2, BLOCKS, rows_out, LANES), sums)
    return grad_input, grad_weight, grad_gain.reshape(DOUT), grad_shift.reshape(DOUT)


def solution(mesh):
    split = Mesh(mesh.devices.reshape(NZ, 2, NY, 2, 2), (Z, XH, Y, XL, C))
    rows = P((Z, XH, Y, XL, C), None)
    shard = P((Z, XH), None)
    return jax.shard_map(
        on_device,
        mesh=split,
        in_specs=(rows, rows, rows, rows, shard, P(), P()),
        out_specs=(rows, shard, P(), P()),
        check_vma=False,
    )
```
